512 devices in a mesh: lon: 64 (over y_hi, z, core), lat: 8 (over y_lo, x).
Axes of the slice: x: 4, y: 8 (y_hi: 4, y_lo: 2; y = y_hi * 2 + y_lo), z: 8, core: 2. Of those that a mesh axis runs over, the one named last changes fastest.
Arguments:
- field_in: bfloat16 [4, 96, 147456], P(None, 'lat', 'lon'), may hold values from -6 to 6
- norm1_gain: float32 [192], replicated, may hold values from 0.25 to 1.75
- qkv_weight: bfloat16 [192, 576], replicated, may hold values from -0.4375 to 0.4375
- proj_weight: bfloat16 [192, 192], replicated, may hold values from -0.4375 to 0.4375
- earth_bias: float32 [16, 2, 6, 20736], P('lat'), may hold values from -4 to 320, as said below
- norm2_gain: float32 [192], replicated, may hold values from 0.25 to 1.75
- fc1_weight: bfloat16 [192, 768], replicated, may hold values from -0.4375 to 0.4375
- fc2_weight: bfloat16 [768, 192], replicated, may hold values from -0.21875 to 0.21875
Outputs:
- block_out: bfloat16 [4, 96, 147456], P(None, 'lat', 'lon')
The draws below stay inside these ranges and needn't reach their ends.
Inputs may be any that keep to these rules, and one draw needn't show every extreme that they name: `earth_bias`: bias table entries.
All inputs are finite; a program needn't handle non-finite values.
Results may differ from the reference program's by a relative error of at most 0.014.
Values may be sent and summed in bfloat16 or wider, within the bound.
A program may use at most 128 MiB of HBM per device.

```python
import jax
import jax.numpy as jnp
from jax import lax

C = 192
HEADS = 6
MLP_UNITS = 768
WIN_LEV = 2
WIN_LAT = 6
WIN_LON = 12
PAIRS = 20736
LEVELS = 4
LAT = 96
LON = 768
NLATW = 16
ZWIN = 2


def draw_earth_bias(key, part):
    shape = (NLATW, ZWIN, HEADS, PAIRS)
    keys = jax.random.split(jax.random.fold_in(key, 7), 1)
    base = jnp.clip(jax.random.normal(keys[0], shape, jnp.float32), -4.0, 4.0)
    return base


def block_levels(stream_key, extent, cuts, low, high):
    level = 1.0
    for axis_at, blocks in cuts:
        heights = jax.random.uniform(jax.random.fold_in(jax.random.fold_in(stream_key, 6), axis_at), (blocks,), jnp.float32, low / len(cuts), high / len(cuts))
        level = level * jnp.repeat(jnp.exp(heights), extent[axis_at] // blocks).reshape((-1,) + (1,) * (len(extent) - 1 - axis_at))
    return level


def gaussian(rng, shape, scale, most, pieces=(), kind=jnp.bfloat16):
    loudness = block_levels(rng, shape, pieces, -0.22, 0.18) if pieces else 1.0
    drawn = jax.random.normal(rng, shape, jnp.float32) * scale * loudness
    return jnp.minimum(jnp.maximum(drawn, -most), most).astype(kind)


def setup_inputs(seed: int = 0) -> dict:
    streams_of = jax.random.split(jax.random.key(seed), 9)
    field_in = gaussian(streams_of[0], (LEVELS, LAT, LON * C), 1.0, 6.0, ((1, 8), (2, 64)))
    norm1_gain = jnp.clip(1.0 + 0.15 * jax.random.normal(streams_of[1], (C,), jnp.float32), 0.25, 1.75)
    qkv_weight = gaussian(streams_of[2], (C, 3 * C), C ** -0.5, 0.4375)
    proj_weight = gaussian(streams_of[3], (C, C), C ** -0.5, 0.4375)
    earth_bias = draw_earth_bias(jax.random.fold_in(streams_of[8], 71), 0)
    norm2_gain = jnp.clip(1.0 + 0.15 * jax.random.normal(streams_of[5], (C,), jnp.float32), 0.25, 1.75)
    fc1_weight = gaussian(streams_of[6], (C, MLP_UNITS), C ** -0.5, 0.4375)
    fc2_weight = gaussian(streams_of[7], (MLP_UNITS, C), MLP_UNITS ** -0.5, 0.21875)
    return dict(field_in=field_in, norm1_gain=norm1_gain, qkv_weight=qkv_weight, proj_weight=proj_weight, earth_bias=earth_bias, norm2_gain=norm2_gain, fc1_weight=fc1_weight, fc2_weight=fc2_weight)


def row_regions(orig, total, padded):
    tail = 4 if padded else 2
    edge = WIN_LAT // 2
    return jnp.where(orig < 0, 3, jnp.where(orig < edge, 2, jnp.where(orig < total - edge, 0, jnp.where(orig < total, 1, tail))))

def level_regions(levels):
    place = jnp.arange(levels)
    return jnp.where(place < levels - 2, 0, jnp.where(place == levels - 2, 1, 2))

def layer_norm(values, gain):
    center = values - lax.optimization_barrier(jnp.mean(values, axis=-1, keepdims=True))
    spread = lax.optimization_barrier(jnp.mean(center * center, axis=-1, keepdims=True))
    return center * lax.rsqrt(spread + 1e-05) * gain.astype(jnp.float32)

def attend(tile, gain, qkv_weight, proj_weight, bias_types, level_lab, row_lab):
    levels, rows, flat = tile.shape
    chans = qkv_weight.shape[0]
    cols = flat // chans
    heads = bias_types.shape[2]
    head_dim = chans // heads
    zwin = levels // WIN_LEV
    rwin = rows // WIN_LAT
    cwin = cols // WIN_LON
    tokens = WIN_LEV * WIN_LAT * WIN_LON
    grid = tile.reshape(zwin, WIN_LEV, rwin, WIN_LAT, cwin, WIN_LON, chans)
    windows = grid.transpose(0, 2, 4, 1, 3, 5, 6).reshape(-1, chans)
    normed = layer_norm(windows.astype(jnp.float32), gain).astype(jnp.bfloat16)
    qkv = jnp.dot(normed, qkv_weight, preferred_element_type=jnp.float32).astype(jnp.bfloat16)
    qkv = lax.optimization_barrier(qkv).astype(jnp.float32)
    qkv = qkv.reshape(zwin, rwin, cwin, tokens, 3, heads, head_dim)
    query = qkv[:, :, :, :, 0]
    keys = qkv[:, :, :, :, 1]
    values = qkv[:, :, :, :, 2]
    scores = jnp.einsum('abcqhd,abckhd->bachqk', query, keys) * head_dim ** (-0.5)
    table = bias_types.reshape(rwin, zwin, heads, tokens, tokens)
    scores = scores + table[:, :, None]
    zlab = level_lab.reshape(zwin, WIN_LEV)
    rlab = row_lab.reshape(rwin, WIN_LAT)
    label = zlab[None, :, :, None, None] * 8 + rlab[:, None, None, :, None] + jnp.zeros((1, 1, 1, 1, WIN_LON), jnp.int32)
    label = label.reshape(rwin, zwin, tokens)
    allowed = label[:, :, :, None] == label[:, :, None, :]
    scores = jnp.where(allowed[:, :, None, None], scores, -1000000000.0)
    probs = jax.nn.softmax(scores, axis=-1).astype(jnp.bfloat16)
    probs = lax.optimization_barrier(probs).astype(jnp.float32)
    mixed = jnp.einsum('bachqk,abckhd->abcqhd', probs, values).astype(jnp.bfloat16).reshape(-1, chans)
    proj = jnp.dot(mixed, proj_weight, preferred_element_type=jnp.float32).astype(jnp.bfloat16)
    back = proj.reshape(zwin, rwin, cwin, WIN_LEV, WIN_LAT, WIN_LON, chans).transpose(0, 3, 1, 4, 2, 5, 6)
    return back.reshape(levels, rows, flat)

def finish(tile, attn, gain, fc1_weight, fc2_weight):
    chans = fc1_weight.shape[0]
    resid = (tile.astype(jnp.float32) + attn.astype(jnp.float32)).astype(jnp.bfloat16)
    resid = lax.optimization_barrier(resid).reshape(-1, chans)
    normed = layer_norm(resid.astype(jnp.float32), gain).astype(jnp.bfloat16)
    hidden = jax.nn.gelu(jnp.dot(normed, fc1_weight, preferred_element_type=jnp.float32)).astype(jnp.bfloat16)
    result = resid.astype(jnp.float32) + jnp.dot(hidden, fc2_weight, preferred_element_type=jnp.float32)
    return result.astype(jnp.bfloat16).reshape(tile.shape)

def reference(field_in, norm1_gain, qkv_weight, proj_weight, earth_bias, norm2_gain, fc1_weight, fc2_weight):
    shift_lanes = WIN_LON // 2 * C
    rolled = jnp.roll(field_in, (-1, -(WIN_LAT // 2), -shift_lanes), axis=(0, 1, 2))
    level_lab = level_regions(LEVELS)
    row_lab = row_regions((jnp.arange(LAT) + WIN_LAT // 2) % LAT, LAT, False).reshape(NLATW, WIN_LAT)
    blocks = rolled.reshape(LEVELS, NLATW, WIN_LAT, LON * C).transpose(1, 0, 2, 3)

    def one_block(items):
        block, table, labels = items
        attn = attend(block, norm1_gain, qkv_weight, proj_weight, table[None], level_lab, labels)
        return finish(block, attn, norm2_gain, fc1_weight, fc2_weight)
    done = lax.map(one_block, (blocks, earth_bias, row_lab))
    done = done.transpose(1, 0, 2, 3).reshape(LEVELS, LAT, LON * C)
    return jnp.roll(done, (1, WIN_LAT // 2, shift_lanes), axis=(0, 1, 2))
```

```python
import functools

import jax
import jax.numpy as jnp
from jax import lax
from jax.experimental import pallas as pl
from jax.experimental.pallas import tpu as pltpu
from jax.sharding import PartitionSpec as P

MESH = pl.DeviceIdType.MESH
BF16 = jnp.bfloat16
F32 = jnp.float32
CH = 192
HEADS = 6
HD = CH // HEADS
TOK = 144
HALF = TOK // 2
LEVEL = ((1, 2), (3, 0))
NEG = -1000000000.0


def dot_nt(a, b):
    return lax.dot_general(a, b, (((1,), (1,)), ((), ())), preferred_element_type=F32)


def dot(a, b):
    return jnp.dot(a, b, preferred_element_type=F32)


def layer_norm(values, gain):
    center = values - jnp.mean(values, axis=-1, keepdims=True)
    spread = jnp.mean(center * center, axis=-1, keepdims=True)
    return center * lax.rsqrt(spread + 1e-05) * gain


def block_kernel(
    lons, lats,
    x_hbm, g1_hbm, wqkv_hbm, wproj_hbm, bias_hbm, g2_hbm, w1_hbm, w2t_hbm,
    out_hbm,
    xin, raw, lin, blo, bhi, frow, xlo, xhi, mixs, xqs, rlo, rhi, orow, stage,
    g1, g2, wqkv, wproj, w1, w2t,
    load_sem, own_sem, send_sem, recv_sem, out_sem,
):
    lon = lax.axis_index("lon")
    lat = lax.axis_index("lat")
    east = lax.rem(lon + 1, lons)
    west = lax.rem(lon + lons - 1, lons)
    south = lax.rem(lat + 1, lats)
    north = lax.rem(lat + lats - 1, lats)

    barrier = pltpu.get_barrier_semaphore()
    for a, b in ((west, lat), (east, lat), (lon, south), (west, south), (east, south), (lon, north)):
        pl.semaphore_signal(barrier, inc=1, device_id={"lon": a, "lat": b}, device_id_type=MESH)

    loads = [
        pltpu.make_async_copy(src, dst, load_sem.at[i])
        for i, (src, dst) in enumerate(
            (
                (bias_hbm, raw), (g1_hbm, g1), (wqkv_hbm, wqkv), (wproj_hbm, wproj),
                (g2_hbm, g2), (w1_hbm, w1), (w2t_hbm, w2t),
            )
        )
    ]
    own = [
        pltpu.make_async_copy(x_hbm.at[3:12, 0:9], xin.at[0, 0:9, 9:18], own_sem.at[0]),
        pltpu.make_async_copy(x_hbm.at[3:12, 9:18], xin.at[1, 0:9, 0:9], own_sem.at[1]),
    ]
    for copy in own + loads:
        copy.start()

    def remote(i, src, dst, a, b):
        return pltpu.make_async_remote_copy(
            src_ref=src, dst_ref=dst, send_sem=send_sem.at[i], recv_sem=recv_sem.at[i],
            device_id={"lon": a, "lat": b}, device_id_type=MESH,
        )

    halo = [
        remote(0, x_hbm.at[3:12, 0:9], xin.at[1, 0:9, 9:18], west, lat),
        remote(1, x_hbm.at[3:12, 9:18], xin.at[0, 0:9, 0:9], east, lat),
        remote(2, x_hbm.at[0:3, 0:9], xin.at[1, 9:12, 9:18], west, north),
        remote(3, x_hbm.at[0:3, 9:18], xin.at[0, 9:12, 0:9], east, north),
        remote(4, x_hbm.at[0:3, 0:9], xin.at[0, 9:12, 9:18], lon, north),
        remote(5, x_hbm.at[0:3, 9:18], xin.at[1, 9:12, 0:9], lon, north),
    ]
    give_back = remote(6, stage.at[9:12], out_hbm.at[0:3], lon, south)

    pl.semaphore_wait(barrier, 6)
    for copy in halo:
        copy.start()

    loads[0].wait()

    def linear(rh, carry):
        base = pl.multiple_of(rh * 324, 4)
        for t in range(162):
            lin[pl.ds(base + 2 * t, 2), :] = raw[rh, :, 128 * t : 128 * t + 128]
        return carry

    lax.fori_loop(0, 12, linear, 0)

    lanes = lax.broadcasted_iota(jnp.int32, (72, 128), 1)
    place = lax.broadcasted_iota(jnp.int32, (72, 128), 0)
    step = lax.rem(place, 6)
    level_q = step // 3
    last = jnp.where(lat == lats - 1, NEG, 0.0).astype(F32)

    def key_level(key):
        return key // 72

    def key_edge(key):
        return lax.rem(key // 12, 6) // 3

    edge_rows = place >= 36

    def penalty(key, odd, zwin):
        row_q = lax.rem(2 * step + odd, 6) // 3
        pen = jnp.where(jnp.logical_and(edge_rows, row_q != key_edge(key)), last, 0.0)
        if zwin:
            pen = pen + jnp.where(level_q != key_level(key), NEG, 0.0)
        return pen

    for zwin in range(2):
        for odd in range(2):
            pen_lo = penalty(lanes, odd, zwin)
            pen_hi = penalty(lanes + 128, odd, zwin)
            for wc in range(12):
                c = 12 * odd + wc
                start = (9 * (c // 8) + c % 8) * 2 + zwin
                this = lin[pl.ds(start, 72, stride=54), :]
                following = lin[pl.ds(start + 2, 72, stride=54), :]
                turn = 16 * (c % 8)
                if turn:
                    this = pltpu.roll(this, 128 - turn, 1)
                    following = pltpu.roll(following, 128 - turn, 1)
                low = jnp.where(lanes < 128 - turn, this, following)
                dest = (zwin * 2 + wc // 6) * 864 + 6 * odd + wc % 6
                blo[pl.ds(dest, 72, stride=12), :] = low + pen_lo
                bhi[pl.ds(dest, 72, stride=12), :] = following + pen_hi

    for copy in loads[1:]:
        copy.wait()
    for copy in own:
        copy.wait()
    for copy in halo:
        copy.wait()

    lane36 = lax.broadcasted_iota(jnp.int32, (36, 128), 1)
    lane18 = lax.broadcasted_iota(jnp.int32, (18, 128), 1)

    def prepare(rwin):
        for ew in range(2):
            tile = xin[ew, 6 * rwin : 6 * rwin + 6].astype(F32)
            frow[pl.ds((ew * 2 + rwin) * 432, 432), :] = tile.reshape(432, 128)
            for zwin in range(2):
                for lev in range(2):
                    base = (ew * 2 + rwin) * 432 + LEVEL[zwin][lev]
                    t0 = frow[pl.ds(base, 36, stride=12), :]
                    t1 = frow[pl.ds(base + 4, 36, stride=12), :]
                    t2 = frow[pl.ds(base + 8, 36, stride=12), :]
                    r1 = pltpu.roll(t1, 64, 1)
                    r2 = pltpu.roll(t2, 64, 1)
                    dest = ((rwin * 2 + zwin) * 2 + ew) * TOK + 72 * lev
                    xlo[pl.ds(dest, 36, stride=2), :] = t0
                    xhi[pl.ds(dest, 36, stride=2), :] = t1
                    xlo[pl.ds(dest + 1, 36, stride=2), :] = jnp.where(lane36 < 64, r1, r2)
                    xhi[pl.ds(dest + 1, 36, stride=2), :] = r2

    sel_k = lax.broadcasted_iota(jnp.int32, (HALF, TOK), 0)
    sel_i = lax.broadcasted_iota(jnp.int32, (HALF, TOK), 1)
    head_of = lax.broadcasted_iota(jnp.int32, (HALF, CH), 1) // HD
    scale = HD ** (-0.5)

    def attend(rwin, zwin, ew):
        win = (rwin * 2 + zwin) * 2 + ew
        half = 1 - ew
        rows = pl.ds(pl.multiple_of(win * TOK, 8), TOK)
        x = jnp.concatenate([xlo[rows, :], xhi[rows, :][:, : CH - 128]], axis=1)
        normed = layer_norm(x, g1[...]).astype(BF16)
        kv = dot(normed, wqkv[:, CH:]).astype(BF16)
        select = jnp.where(sel_i == sel_k + 6 * (sel_k // 6) + 6 * half, 1.0, 0.0).astype(BF16)
        query = dot(dot(select, normed).astype(BF16), wqkv[:, :CH]).astype(BF16).astype(F32)
        stacked = jnp.concatenate(
            [jnp.where(head_of == h, query, 0.0) for h in range(HEADS)], axis=0
        ).astype(BF16)
        scores = dot_nt(stacked, kv[:, :CH]) * scale
        brow = pl.ds(pl.multiple_of(((zwin * 2 + half) * 2 + rwin) * 432, 8), 432)
        scores = scores + jnp.concatenate([blo[brow, :], bhi[brow, :][:, :16]], axis=1)
        top = jnp.max(scores, axis=-1, keepdims=True)
        probs = jnp.exp(scores - top)
        total = jnp.sum(probs, axis=-1, keepdims=True)
        heads = dot(probs.astype(BF16), kv[:, CH:]) / total
        mixed = heads[:HALF]
        for h in range(1, HEADS):
            mixed = jnp.where(head_of == h, heads[h * HALF : (h + 1) * HALF], mixed)
        local = pl.ds(pl.multiple_of((zwin * 2 + ew) * HALF, 8), HALF)
        mixs[local, :] = mixed
        xqs[local, :] = dot(select, x.astype(BF16))

    def attend_all(rwin):
        def body(zwin, carry):
            attend(rwin, zwin, 0)
            attend(rwin, zwin, 1)
            return carry

        lax.fori_loop(0, 2, body, 0)

    def finish(rwin):
        attn = dot(mixs[...].astype(BF16), wproj[...]).astype(BF16).astype(F32)
        resid = (xqs[...] + attn).astype(BF16).astype(F32)
        normed = layer_norm(resid, g2[...]).astype(BF16)
        hidden = jax.nn.gelu(dot(normed, w1[...])).astype(BF16)
        result = resid + dot_nt(hidden, w2t[...])
        rlo[...] = result[:, :128]
        rhi[:, : CH - 128] = result[:, 128:]
        for zwin in range(2):
            for ew in range(2):
                for lev in range(2):
                    base = (zwin * 2 + ew) * HALF + 36 * lev
                    even_lo = rlo[pl.ds(base, 18, stride=2), :]
                    even_hi = rhi[pl.ds(base, 18, stride=2), :]
                    odd_lo = pltpu.roll(rlo[pl.ds(base + 1, 18, stride=2), :], 64, 1)
                    odd_hi = pltpu.roll(rhi[pl.ds(base + 1, 18, stride=2), :], 64, 1)
                    dest = (ew * 12 + 6 * rwin) * 36 + LEVEL[zwin][lev]
                    orow[pl.ds(dest, 18, stride=12), :] = even_lo
                    orow[pl.ds(dest + 4, 18, stride=12), :] = jnp.where(lane18 < 64, even_hi, odd_lo)
                    orow[pl.ds(dest + 8, 18, stride=12), :] = jnp.where(lane18 < 64, odd_lo, odd_hi)
        for ew in range(2):
            tile = orow[pl.ds((ew * 12 + 6 * rwin) * 36, 216), :].reshape(6, 9, 4, 128)
            stage[6 * rwin : 6 * rwin + 6, 9 * ew : 9 * ew + 9] = tile.astype(BF16)

    prepare(0)
    prepare(1)
    attend_all(1)
    finish(1)
    give_back.start()
    attend_all(0)
    finish(0)
    put = pltpu.make_async_copy(stage.at[0:9], out_hbm.at[3:12], out_sem)
    put.start()
    give_back.wait()
    put.wait()


def shards(field_in, g1, wqkv, wproj, bias, g2, w1, w2):
    lons, lats = lax.axis_size("lon"), lax.axis_size("lat")
    x = field_in.reshape(4, 12, 18, 128).transpose(1, 2, 0, 3)
    flat = bias.transpose(0, 2, 1, 3).reshape(12, 2, 20736)
    hbm = pl.BlockSpec(memory_space=pltpu.MemorySpace.HBM)
    out = pl.pallas_call(
        functools.partial(block_kernel, lons, lats),
        out_shape=jax.ShapeDtypeStruct((12, 18, 4, 128), BF16),
        in_specs=[hbm] * 8,
        out_specs=hbm,
        scratch_shapes=[
            pltpu.VMEM((2, 12, 18, 4, 128), BF16),
            pltpu.VMEM((12, 2, 20736), F32),
            pltpu.VMEM((3888, 128), F32),
            pltpu.VMEM((3456, 128), F32),
            pltpu.VMEM((3456, 128), F32),
            pltpu.VMEM((1728, 128), F32),
            pltpu.VMEM((1152, 128), F32),
            pltpu.VMEM((1152, 128), F32),
            pltpu.VMEM((288, CH), F32),
            pltpu.VMEM((288, CH), F32),
            pltpu.VMEM((288, 128), F32),
            pltpu.VMEM((288, 128), F32),
            pltpu.VMEM((864, 128), F32),
            pltpu.VMEM((12, 18, 4, 128), BF16),
            pltpu.VMEM((CH,), F32),
            pltpu.VMEM((CH,), F32),
            pltpu.VMEM((CH, 3 * CH), BF16),
            pltpu.VMEM((CH, CH), BF16),
            pltpu.VMEM((CH, 768), BF16),
            pltpu.VMEM((CH, 768), BF16),
            pltpu.SemaphoreType.DMA((7,)),
            pltpu.SemaphoreType.DMA((2,)),
            pltpu.SemaphoreType.DMA((7,)),
            pltpu.SemaphoreType.DMA((7,)),
            pltpu.SemaphoreType.DMA,
        ],
        compiler_params=pltpu.CompilerParams(
            collective_id=0, has_side_effects=True, vmem_limit_bytes=60 * 1024 * 1024
        ),
        name="swin_block",
    )(x, g1, wqkv, wproj, flat, g2, w1, w2.T)
    return out.transpose(2, 0, 1, 3).reshape(4, 12, 12 * CH)


def solution(mesh):
    in_specs = (P(None, "lat", "lon"), P(), P(), P(), P("lat", None, None, None), P(), P(), P())
    return jax.shard_map(
        shards, mesh=mesh, in_specs=in_specs, out_specs=P(None, "lat", "lon"), check_vma=False
    )
```

```python
import functools

import jax
import jax.numpy as jnp
from jax import lax
from jax.experimental import pallas as pl
from jax.experimental.pallas import tpu as pltpu
from jax.sharding import PartitionSpec as P

MESH = pl.DeviceIdType.MESH
BF16 = jnp.bfloat16
F32 = jnp.float32
CH = 192
HEADS = 6
HD = CH // HEADS
TOK = 144
HALF = TOK // 2
LEVEL = ((1, 2), (3, 0))
NEG = -1000000000.0


def dot_nt(a, b):
    return lax.dot_general(a, b, (((1,), (1,)), ((), ())), preferred_element_type=F32)


def dot(a, b):
    return jnp.dot(a, b, preferred_element_type=F32)


def layer_norm(values, gain):
    center = values - jnp.mean(values, axis=-1, keepdims=True)
    spread = jnp.mean(center * center, axis=-1, keepdims=True)
    return center * lax.rsqrt(spread + 1e-05) * gain


def block_kernel(
    lons, lats,
    x_hbm, g1_hbm, wqkv_hbm, wproj_hbm, bias_hbm, g2_hbm, w1_hbm, w2t_hbm,
    out,
    xin, raw, lin, blo, bhi, frow, xlo, xhi, mixs, xqs, rlo, rhi, orow, back,
    g1, g2, wqkv, wproj, w1, w2t,
    load_sem, own_sem, send_sem, recv_sem,
):
    lon = lax.axis_index("lon")
    lat = lax.axis_index("lat")
    east = lax.rem(lon + 1, lons)
    west = lax.rem(lon + lons - 1, lons)
    south = lax.rem(lat + 1, lats)
    north = lax.rem(lat + lats - 1, lats)

    barrier = pltpu.get_barrier_semaphore()
    for a, b in ((west, lat), (east, lat), (lon, south), (west, south), (east, south), (lon, north)):
        pl.semaphore_signal(barrier, inc=1, device_id={"lon": a, "lat": b}, device_id_type=MESH)

    loads = [
        pltpu.make_async_copy(src, dst, load_sem.at[i])
        for i, (src, dst) in enumerate(
            (
                (bias_hbm, raw), (g1_hbm, g1), (wqkv_hbm, wqkv), (wproj_hbm, wproj),
                (g2_hbm, g2), (w1_hbm, w1), (w2t_hbm, w2t),
            )
        )
    ]
    own = [
        pltpu.make_async_copy(x_hbm.at[3:12, 0:9], xin.at[0, 0:9, 9:18], own_sem.at[0]),
        pltpu.make_async_copy(x_hbm.at[3:12, 9:18], xin.at[1, 0:9, 0:9], own_sem.at[1]),
    ]
    for copy in own + loads:
        copy.start()

    def remote(i, src, dst, a, b):
        return pltpu.make_async_remote_copy(
            src_ref=src, dst_ref=dst, send_sem=send_sem.at[i], recv_sem=recv_sem.at[i],
            device_id={"lon": a, "lat": b}, device_id_type=MESH,
        )

    halo = [
        remote(0, x_hbm.at[9:12, 9:18], xin.at[0, 6:9, 0:9], east, lat),
        remote(1, x_hbm.at[0:3, 9:18], xin.at[0, 9:12, 0:9], east, north),
        remote(2, x_hbm.at[3:9, 9:18], xin.at[0, 0:6, 0:9], east, lat),
        remote(3, x_hbm.at[3:9, 0:9], xin.at[1, 0:6, 9:18], west, lat),
        remote(4, x_hbm.at[9:12, 0:9], xin.at[1, 6:9, 9:18], west, lat),
        remote(5, x_hbm.at[0:3, 0:9], xin.at[1, 9:12, 9:18], west, north),
        remote(6, x_hbm.at[0:3, 9:18], xin.at[1, 9:12, 0:9], lon, north),
        remote(7, x_hbm.at[0:3, 0:9], xin.at[0, 9:12, 9:18], lon, north),
    ]
    needs = {(0, 1): (3,), (1, 1): (4, 5, 6), (1, 0): (0, 1, 7), (0, 0): (2,)}
    give_back = [
        remote(8, back.at[:, 0:9], out.at[0:3, 0:9], lon, south),
        remote(9, back.at[:, 9:18], out.at[0:3, 9:18], lon, south),
    ]

    pl.semaphore_wait(barrier, 6)
    for copy in halo:
        copy.start()

    loads[0].wait()

    def linear(rh, carry):
        base = pl.multiple_of(rh * 324, 4)
        for t in range(162):
            lin[pl.ds(base + 2 * t, 2), :] = raw[rh, :, 128 * t : 128 * t + 128]
        return carry

    lax.fori_loop(0, 12, linear, 0)

    lanes = lax.broadcasted_iota(jnp.int32, (72, 128), 1)
    place = lax.broadcasted_iota(jnp.int32, (72, 128), 0)
    step = lax.rem(place, 6)
    level_q = step // 3
    last = jnp.where(lat == lats - 1, NEG, 0.0).astype(F32)

    def key_level(key):
        return key // 72

    def key_edge(key):
        return lax.rem(key // 12, 6) // 3

    edge_rows = place >= 36

    def penalty(key, odd, zwin):
        row_q = lax.rem(2 * step + odd, 6) // 3
        pen = jnp.where(jnp.logical_and(edge_rows, row_q != key_edge(key)), last, 0.0)
        if zwin:
            pen = pen + jnp.where(level_q != key_level(key), NEG, 0.0)
        return pen

    for zwin in range(2):
        for odd in range(2):
            pen_lo = penalty(lanes, odd, zwin)
            pen_hi = penalty(lanes + 128, odd, zwin)
            for wc in range(12):
                c = 12 * odd + wc
                start = (9 * (c // 8) + c % 8) * 2 + zwin
                this = lin[pl.ds(start, 72, stride=54), :]
                following = lin[pl.ds(start + 2, 72, stride=54), :]
                turn = 16 * (c % 8)
                if turn:
                    this = pltpu.roll(this, 128 - turn, 1)
                    following = pltpu.roll(following, 128 - turn, 1)
                low = jnp.where(lanes < 128 - turn, this, following)
                dest = (zwin * 2 + wc // 6) * 864 + 6 * odd + wc % 6
                blo[pl.ds(dest, 72, stride=12), :] = low + pen_lo
                bhi[pl.ds(dest, 72, stride=12), :] = following + pen_hi

    for copy in loads[1:]:
        copy.wait()
    for copy in own:
        copy.wait()

    lane36 = lax.broadcasted_iota(jnp.int32, (36, 128), 1)
    lane18 = lax.broadcasted_iota(jnp.int32, (18, 128), 1)

    def prepare(rwin, ew):
        tile = xin[ew, 6 * rwin : 6 * rwin + 6].astype(F32)
        frow[pl.ds((ew * 2 + rwin) * 432, 432), :] = tile.reshape(432, 128)
        for zwin in range(2):
            for lev in range(2):
                base = (ew * 2 + rwin) * 432 + LEVEL[zwin][lev]
                t0 = frow[pl.ds(base, 36, stride=12), :]
                t1 = frow[pl.ds(base + 4, 36, stride=12), :]
                t2 = frow[pl.ds(base + 8, 36, stride=12), :]
                r1 = pltpu.roll(t1, 64, 1)
                r2 = pltpu.roll(t2, 64, 1)
                dest = ((rwin * 2 + zwin) * 2 + ew) * TOK + 72 * lev
                xlo[pl.ds(dest, 36, stride=2), :] = t0
                xhi[pl.ds(dest, 36, stride=2), :] = t1
                xlo[pl.ds(dest + 1, 36, stride=2), :] = jnp.where(lane36 < 64, r1, r2)
                xhi[pl.ds(dest + 1, 36, stride=2), :] = r2

    sel_k = lax.broadcasted_iota(jnp.int32, (HALF, TOK), 0)
    sel_i = lax.broadcasted_iota(jnp.int32, (HALF, TOK), 1)
    head_of = lax.broadcasted_iota(jnp.int32, (HALF, CH), 1) // HD
    scale = HD ** (-0.5)

    def attend(rwin, zwin, ew):
        win = (rwin * 2 + zwin) * 2 + ew
        half = 1 - ew
        rows = pl.ds(win * TOK, TOK)
        x = jnp.concatenate([xlo[rows, :], xhi[rows, :][:, : CH - 128]], axis=1)
        normed = layer_norm(x, g1[...]).astype(BF16)
        kv = dot(normed, wqkv[:, CH:]).astype(BF16)
        select = jnp.where(sel_i == sel_k + 6 * (sel_k // 6) + 6 * half, 1.0, 0.0).astype(BF16)
        query = dot(dot(select, normed).astype(BF16), wqkv[:, :CH]).astype(BF16).astype(F32)
        stacked = jnp.concatenate(
            [jnp.where(head_of == h, query, 0.0) for h in range(HEADS)], axis=0
        ).astype(BF16)
        scores = dot_nt(stacked, kv[:, :CH]) * scale
        brow = pl.ds(((zwin * 2 + half) * 2 + rwin) * 432, 432)
        scores = scores + jnp.concatenate([blo[brow, :], bhi[brow, :][:, :16]], axis=1)
        top = jnp.max(scores, axis=-1, keepdims=True)
        probs = jnp.exp(scores - top)
        total = jnp.sum(probs, axis=-1, keepdims=True)
        heads = dot(probs.astype(BF16), kv[:, CH:]) * (1.0 / total)
        mixed = heads[:HALF]
        for h in range(1, HEADS):
            mixed = jnp.where(head_of == h, heads[h * HALF : (h + 1) * HALF], mixed)
        local = pl.ds((ew * 2 + zwin) * HALF, HALF)
        mixs[local, :] = mixed
        xqs[local, :] = dot(select, x.astype(BF16))

    def finish(rwin, ew):
        group = pl.ds(ew * TOK, TOK)
        attn = dot(mixs[group, :].astype(BF16), wproj[...]).astype(BF16).astype(F32)
        resid = (xqs[group, :] + attn).astype(BF16).astype(F32)
        normed = layer_norm(resid, g2[...]).astype(BF16)
        hidden = jax.nn.gelu(dot(normed, w1[...])).astype(BF16)
        result = resid + dot_nt(hidden, w2t[...])
        rlo[group, :] = result[:, :128]
        rhi[group, : CH - 128] = result[:, 128:]
        for zwin in range(2):
            for lev in range(2):
                base = (ew * 2 + zwin) * HALF + 36 * lev
                even_lo = rlo[pl.ds(base, 18, stride=2), :]
                even_hi = rhi[pl.ds(base, 18, stride=2), :]
                odd_lo = pltpu.roll(rlo[pl.ds(base + 1, 18, stride=2), :], 64, 1)
                odd_hi = pltpu.roll(rhi[pl.ds(base + 1, 18, stride=2), :], 64, 1)
                dest = (ew * 12 + 6 * rwin) * 36 + LEVEL[zwin][lev]
                orow[pl.ds(dest, 18, stride=12), :] = even_lo
                orow[pl.ds(dest + 4, 18, stride=12), :] = jnp.where(lane18 < 64, even_hi, odd_lo)
                orow[pl.ds(dest + 8, 18, stride=12), :] = jnp.where(lane18 < 64, odd_lo, odd_hi)
        tile = orow[pl.ds((ew * 12 + 6 * rwin) * 36, 216), :].reshape(6, 9, 4, 128).astype(BF16)
        columns = pl.ds(9 * ew, 9)
        if rwin == 0:
            out[3:9, columns] = tile
        else:
            out[9:12, columns] = tile[:3]
            back[:, columns] = tile[3:]
            give_back[ew].start()

    for rwin, ew in ((0, 1), (1, 1), (1, 0), (0, 0)):
        for i in needs[rwin, ew]:
            halo[i].wait_recv()
        prepare(rwin, ew)
        attend(rwin, 0, ew)
        attend(rwin, 1, ew)
        finish(rwin, ew)
    for copy in halo:
        copy.wait_send()
    for copy in give_back:
        copy.wait()


def shards(field_in, g1, wqkv, wproj, bias, g2, w1, w2):
    lons, lats = lax.axis_size("lon"), lax.axis_size("lat")
    x = field_in.reshape(4, 12, 18, 128).transpose(1, 2, 0, 3)
    flat = bias.transpose(0, 2, 1, 3).reshape(12, 2, 20736)
    hbm = pl.BlockSpec(memory_space=pltpu.MemorySpace.HBM)
    result = pl.pallas_call(
        functools.partial(block_kernel, lons, lats),
        out_shape=pltpu.VMEM((12, 18, 4, 128), BF16),
        in_specs=[hbm] * 8,
        out_specs=pl.BlockSpec(memory_space=pltpu.VMEM),
        scratch_shapes=[
            pltpu.VMEM((2, 12, 18, 4, 128), BF16),
            pltpu.VMEM((12, 2, 20736), F32),
            pltpu.VMEM((3888, 128), F32),
            pltpu.VMEM((3456, 128), F32),
            pltpu.VMEM((3456, 128), F32),
            pltpu.VMEM((1728, 128), F32),
            pltpu.VMEM((1152, 128), F32),
            pltpu.VMEM((1152, 128), F32),
            pltpu.VMEM((288, CH), F32),
            pltpu.VMEM((288, CH), F32),
            pltpu.VMEM((288, 128), F32),
            pltpu.VMEM((288, 128), F32),
            pltpu.VMEM((864, 128), F32),
            pltpu.VMEM((3, 18, 4, 128), BF16),
            pltpu.VMEM((CH,), F32),
            pltpu.VMEM((CH,), F32),
            pltpu.VMEM((CH, 3 * CH), BF16),
            pltpu.VMEM((CH, CH), BF16),
            pltpu.VMEM((CH, 768), BF16),
            pltpu.VMEM((CH, 768), BF16),
            pltpu.SemaphoreType.DMA((7,)),
            pltpu.SemaphoreType.DMA((2,)),
            pltpu.SemaphoreType.DMA((10,)),
            pltpu.SemaphoreType.DMA((10,)),
        ],
        compiler_params=pltpu.CompilerParams(
            collective_id=0, has_side_effects=True, vmem_limit_bytes=60 * 1024 * 1024
        ),
        name="swin_block",
    )(x, g1, wqkv, wproj, flat, g2, w1, w2.T)
    return result.transpose(2, 0, 1, 3).reshape(4, 12, 12 * CH)


def solution(mesh):
    in_specs = (P(None, "lat", "lon"), P(), P(), P(), P("lat", None, None, None), P(), P(), P())
    return jax.shard_map(
        shards, mesh=mesh, in_specs=in_specs, out_specs=P(None, "lat", "lon"), check_vma=False
    )
```

```python
import functools

import jax
import jax.numpy as jnp
from jax import lax
from jax.experimental import pallas as pl
from jax.experimental.pallas import tpu as pltpu
from jax.sharding import PartitionSpec as P

MESH = pl.DeviceIdType.MESH
BF16 = jnp.bfloat16
F32 = jnp.float32
CH = 192
HEADS = 6
HD = CH // HEADS
TOK = 144
HALF = TOK // 2
LEVEL = ((1, 2), (3, 0))
NEG = -1000000000.0


def dot_nt(a, b):
    return lax.dot_general(a, b, (((1,), (1,)), ((), ())), preferred_element_type=F32)


def dot(a, b):
    return jnp.dot(a, b, preferred_element_type=F32)


def layer_norm(values, gain):
    center = values - jnp.mean(values, axis=-1, keepdims=True)
    spread = jnp.mean(center * center, axis=-1, keepdims=True)
    return center * lax.rsqrt(spread + 1e-05) * gain


def block_kernel(
    lons, lats,
    x_hbm, g1_hbm, wqkv_hbm, wproj_hbm, bias_hbm, g2_hbm, w1_hbm, w2t_hbm,
    out,
    xin, raw, lin, blo, bhi, frow, xlo, xhi, mixs, xqs, rlo, rhi, orow, back,
    g1, g2, wqkv, wproj, w1, w2t,
    load_sem, own_sem, send_sem, recv_sem, ready,
):
    lon = lax.axis_index("lon")
    lat = lax.axis_index("lat")
    east = lax.rem(lon + 1, lons)
    west = lax.rem(lon + lons - 1, lons)
    south = lax.rem(lat + 1, lats)
    north = lax.rem(lat + lats - 1, lats)

    barrier = pltpu.get_barrier_semaphore()
    for a, b in ((west, lat), (lon, south), (west, south), (west, north)):
        pl.semaphore_signal(barrier, inc=1, device_id={"lon": a, "lat": b}, device_id_type=MESH)

    loads = [
        pltpu.make_async_copy(src, dst, load_sem.at[i])
        for i, (src, dst) in enumerate(
            (
                (bias_hbm, raw), (g1_hbm, g1), (wqkv_hbm, wqkv), (wproj_hbm, wproj),
                (g2_hbm, g2), (w1_hbm, w1), (w2t_hbm, w2t),
            )
        )
    ]
    own = [
        pltpu.make_async_copy(x_hbm.at[3:12, 0:9], xin.at[0, 0:9, 9:18], own_sem.at[0]),
        pltpu.make_async_copy(x_hbm.at[3:12, 9:18], xin.at[1, 0:9, 0:9], own_sem.at[1]),
    ]
    for copy in own + loads:
        copy.start()

    def remote(i, src, dst, a, b):
        return pltpu.make_async_remote_copy(
            src_ref=src, dst_ref=dst, send_sem=send_sem.at[i], recv_sem=recv_sem.at[i],
            device_id={"lon": a, "lat": b}, device_id_type=MESH,
        )

    halo = [
        remote(0, x_hbm.at[9:12, 9:18], xin.at[0, 6:9, 0:9], east, lat),
        remote(1, x_hbm.at[0:3, 9:18], xin.at[0, 9:12, 0:9], east, north),
        remote(2, x_hbm.at[3:9, 9:18], xin.at[0, 0:6, 0:9], east, lat),
        remote(3, x_hbm.at[3:9, 0:9], xin.at[1, 0:6, 9:18], west, lat),
        remote(4, x_hbm.at[9:12, 0:9], xin.at[1, 6:9, 9:18], west, lat),
        remote(5, x_hbm.at[0:3, 0:9], xin.at[1, 9:12, 9:18], west, north),
        remote(6, x_hbm.at[0:3, 9:18], xin.at[1, 9:12, 0:9], lon, north),
        remote(7, x_hbm.at[0:3, 0:9], xin.at[0, 9:12, 9:18], lon, north),
    ]
    needs = {(0, 1): (3,), (1, 1): (4, 5, 6), (1, 0): (0, 1, 7), (0, 0): (2,)}
    give_back = [
        remote(8, back.at[:, 0:9], out.at[0:3, 0:9], lon, south),
        remote(9, back.at[:, 9:18], out.at[0:3, 9:18], lon, south),
    ]

    pl.semaphore_wait(barrier, 4)
    for i, (a, b) in enumerate(((east, lat), (east, south), (lon, north))):
        pl.semaphore_signal(ready.at[i], inc=1, device_id={"lon": a, "lat": b}, device_id_type=MESH)
    for i in (0, 1, 2, 6, 7):
        halo[i].start()

    def westward():
        pl.semaphore_wait(ready.at[0], 1)
        pl.semaphore_wait(ready.at[1], 1)
        for i in (3, 4, 5):
            halo[i].start()

    across = lax.rem(lon, 16) == 0

    @pl.when(jnp.logical_not(across))
    def _():
        westward()

    loads[0].wait()

    def linear(rh, carry):
        base = pl.multiple_of(rh * 324, 4)
        for t in range(162):
            lin[pl.ds(base + 2 * t, 2), :] = raw[rh, :, 128 * t : 128 * t + 128]
        return carry

    lax.fori_loop(0, 12, linear, 0)

    lanes = lax.broadcasted_iota(jnp.int32, (72, 128), 1)
    place = lax.broadcasted_iota(jnp.int32, (72, 128), 0)
    step = lax.rem(place, 6)
    level_q = step // 3
    last = jnp.where(lat == lats - 1, NEG, 0.0).astype(F32)

    def key_level(key):
        return key // 72

    def key_edge(key):
        return lax.rem(key // 12, 6) // 3

    edge_rows = place >= 36

    def penalty(key, odd, zwin):
        row_q = lax.rem(2 * step + odd, 6) // 3
        pen = jnp.where(jnp.logical_and(edge_rows, row_q != key_edge(key)), last, 0.0)
        if zwin:
            pen = pen + jnp.where(level_q != key_level(key), NEG, 0.0)
        return pen

    for zwin in range(2):
        for odd in range(2):
            pen_lo = penalty(lanes, odd, zwin)
            pen_hi = penalty(lanes + 128, odd, zwin)
            for wc in range(12):
                c = 12 * odd + wc
                start = (9 * (c // 8) + c % 8) * 2 + zwin
                this = lin[pl.ds(start, 72, stride=54), :]
                following = lin[pl.ds(start + 2, 72, stride=54), :]
                turn = 16 * (c % 8)
                if turn:
                    this = pltpu.roll(this, 128 - turn, 1)
                    following = pltpu.roll(following, 128 - turn, 1)
                low = jnp.where(lanes < 128 - turn, this, following)
                dest = (zwin * 2 + wc // 6) * 864 + 6 * odd + wc % 6
                blo[pl.ds(dest, 72, stride=12), :] = low + pen_lo
                bhi[pl.ds(dest, 72, stride=12), :] = following + pen_hi

    for copy in loads[1:]:
        copy.wait()
    for copy in own:
        copy.wait()

    lane36 = lax.broadcasted_iota(jnp.int32, (36, 128), 1)
    lane18 = lax.broadcasted_iota(jnp.int32, (18, 128), 1)

    def prepare(rwin, ew):
        tile = xin[ew, 6 * rwin : 6 * rwin + 6].astype(F32)
        frow[pl.ds((ew * 2 + rwin) * 432, 432), :] = tile.reshape(432, 128)
        for zwin in range(2):
            for lev in range(2):
                base = (ew * 2 + rwin) * 432 + LEVEL[zwin][lev]
                t0 = frow[pl.ds(base, 36, stride=12), :]
                t1 = frow[pl.ds(base + 4, 36, stride=12), :]
                t2 = frow[pl.ds(base + 8, 36, stride=12), :]
                r1 = pltpu.roll(t1, 64, 1)
                r2 = pltpu.roll(t2, 64, 1)
                dest = ((rwin * 2 + zwin) * 2 + ew) * TOK + 72 * lev
                xlo[pl.ds(dest, 36, stride=2), :] = t0
                xhi[pl.ds(dest, 36, stride=2), :] = t1
                xlo[pl.ds(dest + 1, 36, stride=2), :] = jnp.where(lane36 < 64, r1, r2)
                xhi[pl.ds(dest + 1, 36, stride=2), :] = r2

    sel_k = lax.broadcasted_iota(jnp.int32, (HALF, TOK), 0)
    sel_i = lax.broadcasted_iota(jnp.int32, (HALF, TOK), 1)
    head_of = lax.broadcasted_iota(jnp.int32, (HALF, CH), 1) // HD
    scale = HD ** (-0.5)

    def attend(rwin, zwin, ew):
        win = (rwin * 2 + zwin) * 2 + ew
        half = 1 - ew
        rows = pl.ds(win * TOK, TOK)
        x = jnp.concatenate([xlo[rows, :], xhi[rows, :][:, : CH - 128]], axis=1)
        normed = layer_norm(x, g1[...]).astype(BF16)
        kv = dot(normed, wqkv[:, CH:]).astype(BF16)
        select = jnp.where(sel_i == sel_k + 6 * (sel_k // 6) + 6 * half, 1.0, 0.0).astype(BF16)
        query = dot(dot(select, normed).astype(BF16), wqkv[:, :CH]).astype(BF16).astype(F32)
        stacked = jnp.concatenate(
            [jnp.where(head_of == h, query, 0.0) for h in range(HEADS)], axis=0
        ).astype(BF16)
        scores = dot_nt(stacked, kv[:, :CH]) * scale
        brow = pl.ds(((zwin * 2 + half) * 2 + rwin) * 432, 432)
        scores = scores + jnp.concatenate([blo[brow, :], bhi[brow, :][:, :16]], axis=1)
        top = jnp.max(scores, axis=-1, keepdims=True)
        probs = jnp.exp(scores - top)
        total = jnp.sum(probs, axis=-1, keepdims=True)
        heads = dot(probs.astype(BF16), kv[:, CH:]) * (1.0 / total)
        mixed = heads[:HALF]
        for h in range(1, HEADS):
            mixed = jnp.where(head_of == h, heads[h * HALF : (h + 1) * HALF], mixed)
        local = pl.ds((ew * 2 + zwin) * HALF, HALF)
        mixs[local, :] = mixed
        xqs[local, :] = dot(select, x.astype(BF16))

    def finish(rwin, ew):
        group = pl.ds(ew * TOK, TOK)
        attn = dot(mixs[group, :].astype(BF16), wproj[...]).astype(BF16).astype(F32)
        resid = (xqs[group, :] + attn).astype(BF16).astype(F32)
        normed = layer_norm(resid, g2[...]).astype(BF16)
        hidden = jax.nn.gelu(dot(normed, w1[...])).astype(BF16)
        result = resid + dot_nt(hidden, w2t[...])
        rlo[group, :] = result[:, :128]
        rhi[group, : CH - 128] = result[:, 128:]
        for zwin in range(2):
            for lev in range(2):
                base = (ew * 2 + zwin) * HALF + 36 * lev
                even_lo = rlo[pl.ds(base, 18, stride=2), :]
                even_hi = rhi[pl.ds(base, 18, stride=2), :]
                odd_lo = pltpu.roll(rlo[pl.ds(base + 1, 18, stride=2), :], 64, 1)
                odd_hi = pltpu.roll(rhi[pl.ds(base + 1, 18, stride=2), :], 64, 1)
                dest = (ew * 12 + 6 * rwin) * 36 + LEVEL[zwin][lev]
                orow[pl.ds(dest, 18, stride=12), :] = even_lo
                orow[pl.ds(dest + 4, 18, stride=12), :] = jnp.where(lane18 < 64, even_hi, odd_lo)
                orow[pl.ds(dest + 8, 18, stride=12), :] = jnp.where(lane18 < 64, odd_lo, odd_hi)
        tile = orow[pl.ds((ew * 12 + 6 * rwin) * 36, 216), :].reshape(6, 9, 4, 128).astype(BF16)
        columns = pl.ds(9 * ew, 9)
        if rwin == 0:
            out[3:9, columns] = tile
        else:
            out[9:12, columns] = tile[:3]
            back[:, columns] = tile[3:]
            if ew == 0:
                give_back[0].start()

    for rwin, ew in ((0, 1), (1, 1), (1, 0), (0, 0)):
        if (rwin, ew) == (1, 0):
            pl.when(across)(westward)
            pl.semaphore_wait(ready.at[2], 1)
            give_back[1].start()
        for i in needs[rwin, ew]:
            halo[i].wait_recv()
        prepare(rwin, ew)
        attend(rwin, 0, ew)
        attend(rwin, 1, ew)
        finish(rwin, ew)
    for copy in halo:
        copy.wait_send()
    for copy in give_back:
        copy.wait()


def shards(field_in, g1, wqkv, wproj, bias, g2, w1, w2):
    lons, lats = lax.axis_size("lon"), lax.axis_size("lat")
    x = field_in.reshape(4, 12, 18, 128).transpose(1, 2, 0, 3)
    flat = bias.transpose(0, 2, 1, 3).reshape(12, 2, 20736)
    hbm = pl.BlockSpec(memory_space=pltpu.MemorySpace.HBM)
    result = pl.pallas_call(
        functools.partial(block_kernel, lons, lats),
        out_shape=pltpu.VMEM((12, 18, 4, 128), BF16),
        in_specs=[hbm] * 8,
        out_specs=pl.BlockSpec(memory_space=pltpu.VMEM),
        scratch_shapes=[
            pltpu.VMEM((2, 12, 18, 4, 128), BF16),
            pltpu.VMEM((12, 2, 20736), F32),
            pltpu.VMEM((3888, 128), F32),
            pltpu.VMEM((3456, 128), F32),
            pltpu.VMEM((3456, 128), F32),
            pltpu.VMEM((1728, 128), F32),
            pltpu.VMEM((1152, 128), F32),
            pltpu.VMEM((1152, 128), F32),
            pltpu.VMEM((288, CH), F32),
            pltpu.VMEM((288, CH), F32),
            pltpu.VMEM((288, 128), F32),
            pltpu.VMEM((288, 128), F32),
            pltpu.VMEM((864, 128), F32),
            pltpu.VMEM((3, 18, 4, 128), BF16),
            pltpu.VMEM((CH,), F32),
            pltpu.VMEM((CH,), F32),
            pltpu.VMEM((CH, 3 * CH), BF16),
            pltpu.VMEM((CH, CH), BF16),
            pltpu.VMEM((CH, 768), BF16),
            pltpu.VMEM((CH, 768), BF16),
            pltpu.SemaphoreType.DMA((7,)),
            pltpu.SemaphoreType.DMA((2,)),
            pltpu.SemaphoreType.DMA((10,)),
            pltpu.SemaphoreType.DMA((10,)),
            pltpu.SemaphoreType.REGULAR((3,)),
        ],
        compiler_params=pltpu.CompilerParams(
            collective_id=0, has_side_effects=True, vmem_limit_bytes=60 * 1024 * 1024
        ),
        name="swin_block",
    )(x, g1, wqkv, wproj, flat, g2, w1, w2.T)
    return result.transpose(2, 0, 1, 3).reshape(4, 12, 12 * CH)


def solution(mesh):
    in_specs = (P(None, "lat", "lon"), P(), P(), P(), P("lat", None, None, None), P(), P(), P())
    return jax.shard_map(
        shards, mesh=mesh, in_specs=in_specs, out_specs=P(None, "lat", "lon"), check_vma=False
    )
```

```python
import functools

import jax
import jax.numpy as jnp
from jax import lax
from jax.experimental import pallas as pl
from jax.experimental.pallas import tpu as pltpu
from jax.sharding import PartitionSpec as P

MESH = pl.DeviceIdType.MESH
BF16 = jnp.bfloat16
F32 = jnp.float32
CH = 192
HEADS = 6
HD = CH // HEADS
TOK = 144
HALF = TOK // 2
LEVEL = ((1, 2), (3, 0))
NEG = -1000000000.0


def dot_nt(a, b):
    return lax.dot_general(a, b, (((1,), (1,)), ((), ())), preferred_element_type=F32)


def dot(a, b):
    return jnp.dot(a, b, preferred_element_type=F32)


def layer_norm(values, gain):
    center = values - jnp.mean(values, axis=-1, keepdims=True)
    spread = jnp.mean(center * center, axis=-1, keepdims=True)
    return center * lax.rsqrt(spread + 1e-05) * gain


def block_kernel(
    lons, lats,
    x_hbm, g1_hbm, wqkv_hbm, wproj_hbm, bias_hbm, g2_hbm, w1_hbm, w2t_hbm,
    out,
    xin, raw, lin, blo, bhi, frow, xlo, xhi, mixs, xqs, rlo, rhi, orow, back,
    g1, g2, wqkv, wproj, w1, w2t,
    load_sem, own_sem, send_sem, recv_sem, ready,
):
    lon = lax.axis_index("lon")
    lat = lax.axis_index("lat")
    east = lax.rem(lon + 1, lons)
    west = lax.rem(lon + lons - 1, lons)
    south = lax.rem(lat + 1, lats)
    north = lax.rem(lat + lats - 1, lats)

    barrier = pltpu.get_barrier_semaphore()
    for a, b in ((west, lat), (lon, north), (west, south), (west, north)):
        pl.semaphore_signal(barrier, inc=1, device_id={"lon": a, "lat": b}, device_id_type=MESH)

    loads = [
        pltpu.make_async_copy(src, dst, load_sem.at[i])
        for i, (src, dst) in enumerate(
            (
                (bias_hbm, raw), (g1_hbm, g1), (wqkv_hbm, wqkv), (wproj_hbm, wproj),
                (g2_hbm, g2), (w1_hbm, w1), (w2t_hbm, w2t),
            )
        )
    ]
    own = [
        pltpu.make_async_copy(x_hbm.at[3:12, 0:9], xin.at[0, 0:9, 9:18], own_sem.at[0]),
        pltpu.make_async_copy(x_hbm.at[3:12, 9:18], xin.at[1, 0:9, 0:9], own_sem.at[1]),
    ]
    for copy in own + loads:
        copy.start()

    def remote(i, src, dst, a, b):
        return pltpu.make_async_remote_copy(
            src_ref=src, dst_ref=dst, send_sem=send_sem.at[i], recv_sem=recv_sem.at[i],
            device_id={"lon": a, "lat": b}, device_id_type=MESH,
        )

    halo = [
        remote(0, x_hbm.at[9:12, 9:18], xin.at[0, 6:9, 0:9], east, lat),
        remote(1, x_hbm.at[0:3, 9:18], xin.at[0, 9:12, 0:9], east, north),
        remote(2, x_hbm.at[3:9, 9:18], xin.at[0, 0:6, 0:9], east, lat),
        remote(3, x_hbm.at[3:9, 0:9], xin.at[1, 0:6, 9:18], west, lat),
        remote(4, x_hbm.at[9:12, 0:9], xin.at[1, 6:9, 9:18], west, lat),
        remote(5, x_hbm.at[0:3, 0:9], xin.at[1, 9:12, 9:18], west, north),
        remote(6, x_hbm.at[0:3, 9:18], xin.at[1, 9:12, 0:9], lon, north),
        remote(7, x_hbm.at[0:3, 0:9], xin.at[0, 9:12, 9:18], lon, north),
    ]
    needs = (((2,), (0, 1, 7)), ((3,), (4, 5, 6)))

    def give_back(ew):
        columns = pl.ds(9 * ew, 9)
        return remote(8 + ew, back.at[:, columns], out.at[0:3, columns], lon, south)


    pl.semaphore_wait(barrier, 4)
    for i, (a, b) in enumerate(((east, lat), (east, south), (lon, south))):
        pl.semaphore_signal(ready.at[i], inc=1, device_id={"lon": a, "lat": b}, device_id_type=MESH)
    for i in (1, 0, 2):
        halo[i].start()

    def westward():
        pl.semaphore_wait(ready.at[0], 1)
        pl.semaphore_wait(ready.at[1], 1)
        for i in (3, 4, 5):
            halo[i].start()

    loads[0].wait()

    def linear(rh, carry):
        base = pl.multiple_of(rh * 324, 4)
        for t in range(162):
            lin[pl.ds(base + 2 * t, 2), :] = raw[rh, :, 128 * t : 128 * t + 128]
        return carry

    lax.fori_loop(0, 12, linear, 0)

    lanes = lax.broadcasted_iota(jnp.int32, (72, 128), 1)
    place = lax.broadcasted_iota(jnp.int32, (72, 128), 0)
    step = lax.rem(place, 6)
    level_q = step // 3
    last = jnp.where(lat == lats - 1, NEG, 0.0).astype(F32)

    def key_level(key):
        return key // 72

    def key_edge(key):
        return lax.rem(key // 12, 6) // 3

    edge_rows = place >= 36

    def penalty(key, odd, zwin):
        row_q = lax.rem(2 * step + odd, 6) // 3
        pen = jnp.where(jnp.logical_and(edge_rows, row_q != key_edge(key)), last, 0.0)
        if zwin:
            pen = pen + jnp.where(level_q != key_level(key), NEG, 0.0)
        return pen

    for zwin in range(2):
        for odd in range(2):
            pen_lo = penalty(lanes, odd, zwin)
            pen_hi = penalty(lanes + 128, odd, zwin)
            for wc in range(12):
                c = 12 * odd + wc
                start = (9 * (c // 8) + c % 8) * 2 + zwin
                this = lin[pl.ds(start, 72, stride=54), :]
                following = lin[pl.ds(start + 2, 72, stride=54), :]
                turn = 16 * (c % 8)
                if turn:
                    this = pltpu.roll(this, 128 - turn, 1)
                    following = pltpu.roll(following, 128 - turn, 1)
                low = jnp.where(lanes < 128 - turn, this, following)
                dest = (zwin * 2 + wc // 6) * 864 + 6 * odd + wc % 6
                blo[pl.ds(dest, 72, stride=12), :] = low + pen_lo
                bhi[pl.ds(dest, 72, stride=12), :] = following + pen_hi

    pl.semaphore_wait(ready.at[2], 1)
    for i in (6, 7):
        halo[i].start()
    across = lax.rem(lon, 16) == 0

    @pl.when(jnp.logical_not(across))
    def _():
        westward()

    for copy in loads[1:]:
        copy.wait()
    for copy in own:
        copy.wait()

    lane36 = lax.broadcasted_iota(jnp.int32, (36, 128), 1)
    lane18 = lax.broadcasted_iota(jnp.int32, (18, 128), 1)

    def prepare(rwin, ew):
        tile = xin[ew, 6 * rwin : 6 * rwin + 6].astype(F32)
        frow[pl.ds(pl.multiple_of((ew * 2 + rwin) * 432, 8), 432), :] = tile.reshape(432, 128)
        for zwin in range(2):
            for lev in range(2):
                base = (ew * 2 + rwin) * 432 + LEVEL[zwin][lev]
                t0 = frow[pl.ds(base, 36, stride=12), :]
                t1 = frow[pl.ds(base + 4, 36, stride=12), :]
                t2 = frow[pl.ds(base + 8, 36, stride=12), :]
                r1 = pltpu.roll(t1, 64, 1)
                r2 = pltpu.roll(t2, 64, 1)
                dest = ((rwin * 2 + zwin) * 2 + ew) * TOK + 72 * lev
                xlo[pl.ds(dest, 36, stride=2), :] = t0
                xhi[pl.ds(dest, 36, stride=2), :] = t1
                xlo[pl.ds(dest + 1, 36, stride=2), :] = jnp.where(lane36 < 64, r1, r2)
                xhi[pl.ds(dest + 1, 36, stride=2), :] = r2

    sel_k = lax.broadcasted_iota(jnp.int32, (HALF, TOK), 0)
    sel_i = lax.broadcasted_iota(jnp.int32, (HALF, TOK), 1)
    head_of = lax.broadcasted_iota(jnp.int32, (HALF, CH), 1) // HD
    scale = HD ** (-0.5)

    def attend(rwin, zwin, ew):
        win = (rwin * 2 + zwin) * 2 + ew
        half = 1 - ew
        rows = pl.ds(pl.multiple_of(win * TOK, 8), TOK)
        x = jnp.concatenate([xlo[rows, :], xhi[rows, :][:, : CH - 128]], axis=1)
        normed = layer_norm(x, g1[...]).astype(BF16)
        kv = dot(normed, wqkv[:, CH:]).astype(BF16)
        select = jnp.where(sel_i == sel_k + 6 * (sel_k // 6) + 6 * half, 1.0, 0.0).astype(BF16)
        query = dot(dot(select, normed).astype(BF16), wqkv[:, :CH]).astype(BF16).astype(F32)
        stacked = jnp.concatenate(
            [jnp.where(head_of == h, query, 0.0) for h in range(HEADS)], axis=0
        ).astype(BF16)
        scores = dot_nt(stacked, kv[:, :CH]) * scale
        brow = pl.ds(pl.multiple_of(((zwin * 2 + half) * 2 + rwin) * 432, 8), 432)
        scores = scores + jnp.concatenate([blo[brow, :], bhi[brow, :][:, :16]], axis=1)
        top = jnp.max(scores, axis=-1, keepdims=True)
        probs = jnp.exp(scores - top)
        total = jnp.sum(probs, axis=-1, keepdims=True)
        heads = dot(probs.astype(BF16), kv[:, CH:]) * (1.0 / total)
        mixed = heads[:HALF]
        for h in range(1, HEADS):
            mixed = jnp.where(head_of == h, heads[h * HALF : (h + 1) * HALF], mixed)
        local = pl.ds(pl.multiple_of((ew * 2 + zwin) * HALF, 8), HALF)
        mixs[local, :] = mixed
        xqs[local, :] = dot(select, x.astype(BF16))

    def finish(rwin, ew):
        group = pl.ds(pl.multiple_of(ew * TOK, 8), TOK)
        attn = dot(mixs[group, :].astype(BF16), wproj[...]).astype(BF16).astype(F32)
        resid = (xqs[group, :] + attn).astype(BF16).astype(F32)
        normed = layer_norm(resid, g2[...]).astype(BF16)
        hidden = jax.nn.gelu(dot(normed, w1[...])).astype(BF16)
        result = resid + dot_nt(hidden, w2t[...])
        rlo[group, :] = result[:, :128]
        rhi[group, : CH - 128] = result[:, 128:]
        for zwin in range(2):
            for lev in range(2):
                base = (ew * 2 + zwin) * HALF + 36 * lev
                even_lo = rlo[pl.ds(base, 18, stride=2), :]
                even_hi = rhi[pl.ds(base, 18, stride=2), :]
                odd_lo = pltpu.roll(rlo[pl.ds(base + 1, 18, stride=2), :], 64, 1)
                odd_hi = pltpu.roll(rhi[pl.ds(base + 1, 18, stride=2), :], 64, 1)
                dest = (ew * 12 + 6 * rwin) * 36 + LEVEL[zwin][lev]
                orow[pl.ds(dest, 18, stride=12), :] = even_lo
                orow[pl.ds(dest + 4, 18, stride=12), :] = jnp.where(lane18 < 64, even_hi, odd_lo)
                orow[pl.ds(dest + 8, 18, stride=12), :] = jnp.where(lane18 < 64, odd_lo, odd_hi)
        tile = orow[pl.ds(pl.multiple_of((ew * 12 + 6 * rwin) * 36, 8), 216), :].reshape(6, 9, 4, 128).astype(BF16)
        columns = pl.ds(9 * ew, 9)
        if rwin == 0:
            out[3:9, columns] = tile
        else:
            out[9:12, columns] = tile[:3]
            back[:, columns] = tile[3:]
            give_back(ew).start()

    def group(rwin, ew):
        for side in range(2):

            @pl.when(ew == side)
            def _(side=side):
                for i in needs[side][rwin]:
                    halo[i].wait_recv()

        prepare(rwin, ew)
        attend(rwin, 0, ew)
        attend(rwin, 1, ew)
        finish(rwin, ew)

    early = jnp.where(across, 1, 0)
    group(0, early)
    group(1, early)
    pl.when(across)(westward)
    group(1, 1 - early)
    group(0, 1 - early)
    for copy in halo:
        copy.wait_send()
    for ew in range(2):
        give_back(ew).wait()


def shards(field_in, g1, wqkv, wproj, bias, g2, w1, w2):
    lons, lats = lax.axis_size("lon"), lax.axis_size("lat")
    x = field_in.reshape(4, 12, 18, 128).transpose(1, 2, 0, 3)
    flat = bias.transpose(0, 2, 1, 3).reshape(12, 2, 20736)
    hbm = pl.BlockSpec(memory_space=pltpu.MemorySpace.HBM)
    result = pl.pallas_call(
        functools.partial(block_kernel, lons, lats),
        out_shape=pltpu.VMEM((12, 18, 4, 128), BF16),
        in_specs=[hbm] * 8,
        out_specs=pl.BlockSpec(memory_space=pltpu.VMEM),
        scratch_shapes=[
            pltpu.VMEM((2, 12, 18, 4, 128), BF16),
            pltpu.VMEM((12, 2, 20736), F32),
            pltpu.VMEM((3888, 128), F32),
            pltpu.VMEM((3456, 128), F32),
            pltpu.VMEM((3456, 128), F32),
            pltpu.VMEM((1728, 128), F32),
            pltpu.VMEM((1152, 128), F32),
            pltpu.VMEM((1152, 128), F32),
            pltpu.VMEM((288, CH), F32),
            pltpu.VMEM((288, CH), F32),
            pltpu.VMEM((288, 128), F32),
            pltpu.VMEM((288, 128), F32),
            pltpu.VMEM((864, 128), F32),
            pltpu.VMEM((3, 18, 4, 128), BF16),
            pltpu.VMEM((CH,), F32),
            pltpu.VMEM((CH,), F32),
            pltpu.VMEM((CH, 3 * CH), BF16),
            pltpu.VMEM((CH, CH), BF16),
            pltpu.VMEM((CH, 768), BF16),
            pltpu.VMEM((CH, 768), BF16),
            pltpu.SemaphoreType.DMA((7,)),
            pltpu.SemaphoreType.DMA((2,)),
            pltpu.SemaphoreType.DMA((10,)),
            pltpu.SemaphoreType.DMA((10,)),
            pltpu.SemaphoreType.REGULAR((3,)),
        ],
        compiler_params=pltpu.CompilerParams(
            collective_id=0, has_side_effects=True, vmem_limit_bytes=60 * 1024 * 1024
        ),
        name="swin_block",
    )(x, g1, wqkv, wproj, flat, g2, w1, w2.T)
    return result.transpose(2, 0, 1, 3).reshape(4, 12, 12 * CH)


def solution(mesh):
    in_specs = (P(None, "lat", "lon"), P(), P(), P(), P("lat", None, None, None), P(), P(), P())
    return jax.shard_map(
        shards, mesh=mesh, in_specs=in_specs, out_specs=P(None, "lat", "lon"), check_vma=False
    )
```

```python
import functools

import jax
import jax.numpy as jnp
from jax import lax
from jax.experimental import pallas as pl
from jax.experimental.pallas import tpu as pltpu
from jax.sharding import PartitionSpec as P

MESH = pl.DeviceIdType.MESH
BF16 = jnp.bfloat16
F32 = jnp.float32
CH = 192
HEADS = 6
HD = CH // HEADS
TOK = 144
HALF = TOK // 2
LEVEL = ((1, 2), (3, 0))
NEG = -1000000000.0
LOG2E = 1.4426950408889634


def dot_nt(a, b):
    return lax.dot_general(a, b, (((1,), (1,)), ((), ())), preferred_element_type=F32)


def dot(a, b):
    return jnp.dot(a, b, preferred_element_type=F32)


def layer_norm(values, gain):
    center = values - jnp.mean(values, axis=-1, keepdims=True)
    spread = jnp.mean(center * center, axis=-1, keepdims=True)
    return center * lax.rsqrt(spread + 1e-05) * gain


def block_kernel(
    lons, lats,
    x_hbm, g1_hbm, wqkv_hbm, wproj_hbm, bias_hbm, g2_hbm, w1_hbm, w2t_hbm,
    out,
    xin, raw, lin, blo, bhi, fq, qlo, qhi, stack, qst, frow, xlo, xhi, mixs, rlo, rhi, orow, back,
    g1, g2, wqkv, wproj, w1, w2t,
    load_sem, own_sem, send_sem, recv_sem, ready,
):
    lon = lax.axis_index("lon")
    lat = lax.axis_index("lat")
    east = lax.rem(lon + 1, lons)
    west = lax.rem(lon + lons - 1, lons)
    south = lax.rem(lat + 1, lats)
    north = lax.rem(lat + lats - 1, lats)

    barrier = pltpu.get_barrier_semaphore()
    for a, b in ((west, lat), (lon, north), (west, south), (west, north)):
        pl.semaphore_signal(barrier, inc=1, device_id={"lon": a, "lat": b}, device_id_type=MESH)

    loads = [
        pltpu.make_async_copy(src, dst, load_sem.at[i])
        for i, (src, dst) in enumerate(
            (
                (bias_hbm, raw), (g1_hbm, g1), (wqkv_hbm, wqkv), (wproj_hbm, wproj),
                (g2_hbm, g2), (w1_hbm, w1), (w2t_hbm, w2t),
            )
        )
    ]
    own = [
        pltpu.make_async_copy(x_hbm.at[3:12, 0:9], xin.at[0, 0:9, 9:18], own_sem.at[0]),
        pltpu.make_async_copy(x_hbm.at[3:12, 9:18], xin.at[1, 0:9, 0:9], own_sem.at[1]),
    ]
    for copy in own + loads:
        copy.start()

    def remote(i, src, dst, a, b):
        return pltpu.make_async_remote_copy(
            src_ref=src, dst_ref=dst, send_sem=send_sem.at[i], recv_sem=recv_sem.at[i],
            device_id={"lon": a, "lat": b}, device_id_type=MESH,
        )

    halo = [
        remote(0, x_hbm.at[9:12, 9:18], xin.at[0, 6:9, 0:9], east, lat),
        remote(1, x_hbm.at[0:3, 9:18], xin.at[0, 9:12, 0:9], east, north),
        remote(2, x_hbm.at[3:9, 9:18], xin.at[0, 0:6, 0:9], east, lat),
        remote(3, x_hbm.at[3:9, 0:9], xin.at[1, 0:6, 9:18], west, lat),
        remote(4, x_hbm.at[9:12, 0:9], xin.at[1, 6:9, 9:18], west, lat),
        remote(5, x_hbm.at[0:3, 0:9], xin.at[1, 9:12, 9:18], west, north),
        remote(6, x_hbm.at[0:3, 9:18], xin.at[1, 9:12, 0:9], lon, north),
        remote(7, x_hbm.at[0:3, 0:9], xin.at[0, 9:12, 9:18], lon, north),
    ]
    query_needs = (((), (7,)), ((), (6,)))
    key_needs = (((2,), (0, 1)), ((3,), (4, 5)))

    def give_back(ew):
        columns = pl.ds(9 * ew, 9)
        return remote(8 + ew, back.at[:, columns], out.at[0:3, columns], lon, south)


    pl.semaphore_wait(barrier, 4)
    for i, (a, b) in enumerate(((east, lat), (east, south), (lon, south))):
        pl.semaphore_signal(ready.at[i], inc=1, device_id={"lon": a, "lat": b}, device_id_type=MESH)
    for i in (1, 0, 2):
        halo[i].start()

    def westward():
        pl.semaphore_wait(ready.at[0], 1)
        pl.semaphore_wait(ready.at[1], 1)
        for i in (3, 4, 5):
            halo[i].start()

    loads[0].wait()

    def linear(rh, carry):
        base = pl.multiple_of(rh * 324, 4)
        for t in range(162):
            lin[pl.ds(base + 2 * t, 2), :] = raw[rh, :, 128 * t : 128 * t + 128]
        return carry

    lax.fori_loop(0, 12, linear, 0)

    lanes = lax.broadcasted_iota(jnp.int32, (72, 128), 1)
    place = lax.broadcasted_iota(jnp.int32, (72, 128), 0)
    step = lax.rem(place, 6)
    level_q = step // 3
    last = jnp.where(lat == lats - 1, NEG, 0.0).astype(F32)

    def key_level(key):
        return key // 72

    def key_edge(key):
        return lax.rem(key // 12, 6) // 3

    edge_rows = place >= 36

    def penalty(key, odd, zwin):
        row_q = lax.rem(2 * step + odd, 6) // 3
        pen = jnp.where(jnp.logical_and(edge_rows, row_q != key_edge(key)), last, 0.0)
        if zwin:
            pen = pen + jnp.where(level_q != key_level(key), NEG, 0.0)
        return pen

    for zwin in range(2):
        for odd in range(2):
            pen_lo = penalty(lanes, odd, zwin)
            pen_hi = penalty(lanes + 128, odd, zwin)
            for wc in range(12):
                c = 12 * odd + wc
                start = (9 * (c // 8) + c % 8) * 2 + zwin
                this = lin[pl.ds(start, 72, stride=54), :]
                following = lin[pl.ds(start + 2, 72, stride=54), :]
                turn = 16 * (c % 8)
                if turn:
                    this = pltpu.roll(this, 128 - turn, 1)
                    following = pltpu.roll(following, 128 - turn, 1)
                low = jnp.where(lanes < 128 - turn, this, following)
                dest = (zwin * 2 + wc // 6) * 864 + 6 * odd + wc % 6
                blo[pl.ds(dest, 72, stride=12), :] = low * LOG2E + pen_lo
                bhi[pl.ds(dest, 72, stride=12), :] = following * LOG2E + pen_hi

    pl.semaphore_wait(ready.at[2], 1)
    for i in (6, 7):
        halo[i].start()
    across = lax.rem(lon, 16) == 0

    @pl.when(jnp.logical_not(across))
    def _():
        westward()

    for copy in loads[1:]:
        copy.wait()
    for copy in own:
        copy.wait()

    lane36 = lax.broadcasted_iota(jnp.int32, (36, 128), 1)
    lane18 = lax.broadcasted_iota(jnp.int32, (18, 128), 1)

    head_of = lax.broadcasted_iota(jnp.int32, (HALF, CH), 1) // HD

    def queries(rwin, ew):
        own_tiles = pl.ds(9 - 9 * ew, 9)
        tile = xin[ew, 6 * rwin : 6 * rwin + 6, own_tiles].astype(F32)
        fq[rwin * 216 : rwin * 216 + 216, :] = tile.reshape(216, 128)
        for zwin in range(2):
            for lev in range(2):
                base = rwin * 216 + LEVEL[zwin][lev]
                t0 = fq[pl.ds(base, 18, stride=12), :]
                t1 = fq[pl.ds(base + 4, 18, stride=12), :]
                t2 = fq[pl.ds(base + 8, 18, stride=12), :]
                r1 = pltpu.roll(t1, 64, 1)
                r2 = pltpu.roll(t2, 64, 1)
                dest = rwin * TOK + zwin * HALF + 36 * lev
                qlo[pl.ds(dest, 18, stride=2), :] = t0
                qhi[pl.ds(dest, 18, stride=2), :] = t1
                qlo[pl.ds(dest + 1, 18, stride=2), :] = jnp.where(lane18 < 64, r1, r2)
                qhi[pl.ds(dest + 1, 18, stride=2), :] = r2
        normed = layer_norm(tokens(qlo, qhi, rwin * TOK, TOK), g1[...]).astype(BF16)
        query = dot(normed, wqkv[:, :CH]) * (HD ** (-0.5) * LOG2E)
        for zwin in range(2):
            part = query[zwin * HALF : (zwin + 1) * HALF]
            for h in range(HEADS):
                stack[pl.ds(h * HALF, HALF), :] = jnp.where(head_of == h, part, 0.0)
            qst[rwin, zwin] = stack[...].astype(BF16)

    def tokens(low, high, start, size):
        return jnp.concatenate([low[start : start + size, :], high[start : start + size, : CH - 128]], axis=1)

    def attend(rwin, ew):
        tile = xin[ew, 6 * rwin : 6 * rwin + 6].astype(F32)
        frow[rwin * 432 : rwin * 432 + 432, :] = tile.reshape(432, 128)
        for zwin in range(2):
            for lev in range(2):
                base = rwin * 432 + LEVEL[zwin][lev]
                t0 = frow[pl.ds(base, 36, stride=12), :]
                t1 = frow[pl.ds(base + 4, 36, stride=12), :]
                t2 = frow[pl.ds(base + 8, 36, stride=12), :]
                r1 = pltpu.roll(t1, 64, 1)
                r2 = pltpu.roll(t2, 64, 1)
                dest = (rwin * 2 + zwin) * TOK + 72 * lev
                xlo[pl.ds(dest, 36, stride=2), :] = t0
                xhi[pl.ds(dest, 36, stride=2), :] = t1
                xlo[pl.ds(dest + 1, 36, stride=2), :] = jnp.where(lane36 < 64, r1, r2)
                xhi[pl.ds(dest + 1, 36, stride=2), :] = r2
        normed = layer_norm(tokens(xlo, xhi, rwin * 2 * TOK, 2 * TOK), g1[...]).astype(BF16)
        kv = dot(normed, wqkv[:, CH:]).astype(BF16)
        for zwin in range(2):
            mine = kv[zwin * TOK : (zwin + 1) * TOK]
            scores = dot_nt(qst[rwin, zwin], mine[:, :CH])
            brow = pl.ds(pl.multiple_of(((zwin * 2 + 1 - ew) * 2 + rwin) * 432, 8), 432)
            scores = scores + jnp.concatenate([blo[brow, :], bhi[brow, :][:, :16]], axis=1)
            top = jnp.max(scores, axis=-1, keepdims=True)
            probs = jnp.exp2(scores - top)
            total = jnp.sum(probs, axis=-1, keepdims=True)
            heads = dot(probs.astype(BF16), mine[:, CH:])
            mixed, norm = heads[:HALF], jnp.broadcast_to(total[:HALF], (HALF, CH))
            for h in range(1, HEADS):
                mixed = jnp.where(head_of == h, heads[h * HALF : (h + 1) * HALF], mixed)
                norm = jnp.where(head_of == h, total[h * HALF : (h + 1) * HALF], norm)
            mixs[rwin, zwin * HALF : (zwin + 1) * HALF, :] = mixed / norm

    def finish(rwin, ew):
        attn = dot(mixs[rwin].astype(BF16), wproj[...]).astype(BF16).astype(F32)
        resid = (tokens(qlo, qhi, rwin * TOK, TOK) + attn).astype(BF16).astype(F32)
        normed = layer_norm(resid, g2[...]).astype(BF16)
        hidden = jax.nn.gelu(dot(normed, w1[...])).astype(BF16)
        result = resid + dot_nt(hidden, w2t[...])
        rlo[...] = result[:, :128]
        rhi[:, : CH - 128] = result[:, 128:]
        for zwin in range(2):
            for lev in range(2):
                base = zwin * HALF + 36 * lev
                even_lo = rlo[pl.ds(base, 18, stride=2), :]
                even_hi = rhi[pl.ds(base, 18, stride=2), :]
                odd_lo = pltpu.roll(rlo[pl.ds(base + 1, 18, stride=2), :], 64, 1)
                odd_hi = pltpu.roll(rhi[pl.ds(base + 1, 18, stride=2), :], 64, 1)
                dest = LEVEL[zwin][lev]
                orow[pl.ds(dest, 18, stride=12), :] = even_lo
                orow[pl.ds(dest + 4, 18, stride=12), :] = jnp.where(lane18 < 64, even_hi, odd_lo)
                orow[pl.ds(dest + 8, 18, stride=12), :] = jnp.where(lane18 < 64, odd_lo, odd_hi)
        tile = orow[...].reshape(6, 9, 4, 128).astype(BF16)
        columns = pl.ds(9 * ew, 9)
        if rwin == 0:
            out[3:9, columns] = tile
        else:
            out[9:12, columns] = tile[:3]
            back[:, columns] = tile[3:]
            give_back(ew).start()

    def arrive(which, rwin, ew):
        for side in range(2):

            @pl.when(ew == side)
            def _(side=side):
                for i in which[side][rwin]:
                    halo[i].wait_recv()

    early = jnp.where(across, 1, 0)
    late = 1 - early
    for rwin in range(2):
        arrive(query_needs, rwin, early)
        queries(rwin, early)
        arrive(key_needs, rwin, early)
        attend(rwin, early)
        finish(rwin, early)
    for rwin in (1, 0):
        arrive(query_needs, rwin, late)
        queries(rwin, late)
    pl.when(across)(westward)
    for rwin in (1, 0):
        arrive(key_needs, rwin, late)
        attend(rwin, late)
        finish(rwin, late)
    for copy in halo:
        copy.wait_send()
    for ew in range(2):
        give_back(ew).wait()


def shards(field_in, g1, wqkv, wproj, bias, g2, w1, w2):
    lons, lats = lax.axis_size("lon"), lax.axis_size("lat")
    x = field_in.reshape(4, 12, 18, 128).transpose(1, 2, 0, 3)
    flat = bias.transpose(0, 2, 1, 3).reshape(12, 2, 20736)
    hbm = pl.BlockSpec(memory_space=pltpu.MemorySpace.HBM)
    result = pl.pallas_call(
        functools.partial(block_kernel, lons, lats),
        out_shape=pltpu.VMEM((12, 18, 4, 128), BF16),
        in_specs=[hbm] * 8,
        out_specs=pl.BlockSpec(memory_space=pltpu.VMEM),
        scratch_shapes=[
            pltpu.VMEM((2, 12, 18, 4, 128), BF16),
            pltpu.VMEM((12, 2, 20736), F32),
            pltpu.VMEM((3888, 128), F32),
            pltpu.VMEM((3456, 128), F32),
            pltpu.VMEM((3456, 128), F32),
            pltpu.VMEM((432, 128), F32),
            pltpu.VMEM((288, 128), F32),
            pltpu.VMEM((288, 128), F32),
            pltpu.VMEM((432, CH), F32),
            pltpu.VMEM((2, 2, 432, CH), BF16),
            pltpu.VMEM((864, 128), F32),
            pltpu.VMEM((576, 128), F32),
            pltpu.VMEM((576, 128), F32),
            pltpu.VMEM((2, TOK, CH), F32),
            pltpu.VMEM((TOK, 128), F32),
            pltpu.VMEM((TOK, 128), F32),
            pltpu.VMEM((216, 128), F32),
            pltpu.VMEM((3, 18, 4, 128), BF16),
            pltpu.VMEM((CH,), F32),
            pltpu.VMEM((CH,), F32),
            pltpu.VMEM((CH, 3 * CH), BF16),
            pltpu.VMEM((CH, CH), BF16),
            pltpu.VMEM((CH, 768), BF16),
            pltpu.VMEM((CH, 768), BF16),
            pltpu.SemaphoreType.DMA((7,)),
            pltpu.SemaphoreType.DMA((2,)),
            pltpu.SemaphoreType.DMA((10,)),
            pltpu.SemaphoreType.DMA((10,)),
            pltpu.SemaphoreType.REGULAR((3,)),
        ],
        compiler_params=pltpu.CompilerParams(
            collective_id=0, has_side_effects=True, vmem_limit_bytes=60 * 1024 * 1024
        ),
        name="swin_block",
    )(x, g1, wqkv, wproj, flat, g2, w1, w2.T)
    return result.transpose(2, 0, 1, 3).reshape(4, 12, 12 * CH)


def solution(mesh):
    in_specs = (P(None, "lat", "lon"), P(), P(), P(), P("lat", None, None, None), P(), P(), P())
    return jax.shard_map(
        shards, mesh=mesh, in_specs=in_specs, out_specs=P(None, "lat", "lon"), check_vma=False
    )
```

```python
import functools

import jax
import jax.numpy as jnp
from jax import lax
from jax.experimental import pallas as pl
from jax.experimental.pallas import tpu as pltpu
from jax.sharding import PartitionSpec as P

MESH = pl.DeviceIdType.MESH
BF16 = jnp.bfloat16
F32 = jnp.float32
CH = 192
HEADS = 6
HD = CH // HEADS
TOK = 144
HALF = TOK // 2
LEVEL = ((1, 2), (3, 0))
NEG = -1000000000.0
LOG2E = 1.4426950408889634


def dot_nt(a, b):
    return lax.dot_general(a, b, (((1,), (1,)), ((), ())), preferred_element_type=F32)


def dot(a, b):
    return jnp.dot(a, b, preferred_element_type=F32)


def row_mean(values):
    mean = dot(values.astype(BF16), jnp.ones((CH, 128), BF16)) * (1.0 / CH)
    return jnp.concatenate([mean, mean[:, : CH - 128]], axis=1)


def layer_norm(values, gain):
    center = values - row_mean(values)
    spread = row_mean(center * center)
    return center * lax.rsqrt(spread + 1e-05) * gain


def block_kernel(
    lons, lats,
    x_hbm, g1_hbm, wqkv_hbm, wproj_hbm, bias_hbm, g2_hbm, w1_hbm, w2t_hbm,
    out,
    xin, raw, lin, blo, bhi, fq, qlo, qhi, stack, qst, frow, xlo, xhi, mixs, rlo, rhi, orow, back,
    g1, g2, wqkv, wproj, w1, w2t,
    load_sem, own_sem, send_sem, recv_sem, ready,
):
    lon = lax.axis_index("lon")
    lat = lax.axis_index("lat")
    east = lax.rem(lon + 1, lons)
    west = lax.rem(lon + lons - 1, lons)
    south = lax.rem(lat + 1, lats)
    north = lax.rem(lat + lats - 1, lats)

    barrier = pltpu.get_barrier_semaphore()
    for a, b in ((west, lat), (lon, north), (west, south), (west, north)):
        pl.semaphore_signal(barrier, inc=1, device_id={"lon": a, "lat": b}, device_id_type=MESH)

    loads = [
        pltpu.make_async_copy(src, dst, load_sem.at[i])
        for i, (src, dst) in enumerate(
            (
                (bias_hbm, raw), (g1_hbm, g1), (wqkv_hbm, wqkv), (wproj_hbm, wproj),
                (g2_hbm, g2), (w1_hbm, w1), (w2t_hbm, w2t),
            )
        )
    ]
    own = [
        pltpu.make_async_copy(x_hbm.at[3:12, 0:9], xin.at[0, 0:9, 9:18], own_sem.at[0]),
        pltpu.make_async_copy(x_hbm.at[3:12, 9:18], xin.at[1, 0:9, 0:9], own_sem.at[1]),
    ]
    for copy in own + loads:
        copy.start()

    def remote(i, src, dst, a, b):
        return pltpu.make_async_remote_copy(
            src_ref=src, dst_ref=dst, send_sem=send_sem.at[i], recv_sem=recv_sem.at[i],
            device_id={"lon": a, "lat": b}, device_id_type=MESH,
        )

    halo = [
        remote(0, x_hbm.at[9:12, 9:18], xin.at[0, 6:9, 0:9], east, lat),
        remote(1, x_hbm.at[0:3, 9:18], xin.at[0, 9:12, 0:9], east, north),
        remote(2, x_hbm.at[3:9, 9:18], xin.at[0, 0:6, 0:9], east, lat),
        remote(3, x_hbm.at[3:9, 0:9], xin.at[1, 0:6, 9:18], west, lat),
        remote(4, x_hbm.at[9:12, 0:9], xin.at[1, 6:9, 9:18], west, lat),
        remote(5, x_hbm.at[0:3, 0:9], xin.at[1, 9:12, 9:18], west, north),
        remote(6, x_hbm.at[0:3, 9:18], xin.at[1, 9:12, 0:9], lon, north),
        remote(7, x_hbm.at[0:3, 0:9], xin.at[0, 9:12, 9:18], lon, north),
    ]
    query_needs = (((), (7,)), ((), (6,)))
    key_needs = (((2,), (0, 1)), ((3,), (4, 5)))

    def give_back(ew):
        columns = pl.ds(9 * ew, 9)
        return remote(8 + ew, back.at[:, columns], out.at[0:3, columns], lon, south)


    pl.semaphore_wait(barrier, 4)
    for i, (a, b) in enumerate(((east, lat), (east, south), (lon, south))):
        pl.semaphore_signal(ready.at[i], inc=1, device_id={"lon": a, "lat": b}, device_id_type=MESH)
    for i in (1, 0, 2):
        halo[i].start()

    def westward():
        pl.semaphore_wait(ready.at[0], 1)
        pl.semaphore_wait(ready.at[1], 1)
        for i in (3, 4, 5):
            halo[i].start()

    loads[0].wait()

    def linear(rh, carry):
        base = pl.multiple_of(rh * 324, 4)
        for t in range(162):
            lin[pl.ds(base + 2 * t, 2), :] = raw[rh, :, 128 * t : 128 * t + 128]
        return carry

    lax.fori_loop(0, 12, linear, 0)

    lanes = lax.broadcasted_iota(jnp.int32, (72, 128), 1)
    place = lax.broadcasted_iota(jnp.int32, (72, 128), 0)
    step = lax.rem(place, 6)
    level_q = step // 3
    last = jnp.where(lat == lats - 1, NEG, 0.0).astype(F32)

    def key_level(key):
        return key // 72

    def key_edge(key):
        return lax.rem(key // 12, 6) // 3

    edge_rows = place >= 36

    def penalty(key, odd, zwin):
        row_q = lax.rem(2 * step + odd, 6) // 3
        pen = jnp.where(jnp.logical_and(edge_rows, row_q != key_edge(key)), last, 0.0)
        if zwin:
            pen = pen + jnp.where(level_q != key_level(key), NEG, 0.0)
        return pen

    for zwin in range(2):
        for odd in range(2):
            pen_lo = penalty(lanes, odd, zwin)
            pen_hi = penalty(lanes + 128, odd, zwin)
            for wc in range(12):
                c = 12 * odd + wc
                start = (9 * (c // 8) + c % 8) * 2 + zwin
                this = lin[pl.ds(start, 72, stride=54), :]
                following = lin[pl.ds(start + 2, 72, stride=54), :]
                turn = 16 * (c % 8)
                if turn:
                    this = pltpu.roll(this, 128 - turn, 1)
                    following = pltpu.roll(following, 128 - turn, 1)
                low = jnp.where(lanes < 128 - turn, this, following)
                dest = (zwin * 2 + wc // 6) * 864 + 6 * odd + wc % 6
                blo[pl.ds(dest, 72, stride=12), :] = low * LOG2E + pen_lo
                bhi[pl.ds(dest, 72, stride=12), :] = following * LOG2E + pen_hi

    pl.semaphore_wait(ready.at[2], 1)
    for i in (6, 7):
        halo[i].start()
    across = lax.rem(lon, 16) == 0

    @pl.when(jnp.logical_not(across))
    def _():
        westward()

    for copy in loads[1:]:
        copy.wait()
    for copy in own:
        copy.wait()

    lane36 = lax.broadcasted_iota(jnp.int32, (36, 128), 1)
    lane18 = lax.broadcasted_iota(jnp.int32, (18, 128), 1)

    head_of = lax.broadcasted_iota(jnp.int32, (HALF, CH), 1) // HD

    def queries(rwin, ew):
        own_tiles = pl.ds(9 - 9 * ew, 9)
        tile = xin[ew, 6 * rwin : 6 * rwin + 6, own_tiles].astype(F32)
        fq[rwin * 216 : rwin * 216 + 216, :] = tile.reshape(216, 128)
        for zwin in range(2):
            for lev in range(2):
                base = rwin * 216 + LEVEL[zwin][lev]
                t0 = fq[pl.ds(base, 18, stride=12), :]
                t1 = fq[pl.ds(base + 4, 18, stride=12), :]
                t2 = fq[pl.ds(base + 8, 18, stride=12), :]
                r1 = pltpu.roll(t1, 64, 1)
                r2 = pltpu.roll(t2, 64, 1)
                dest = rwin * TOK + zwin * HALF + 36 * lev
                qlo[pl.ds(dest, 18, stride=2), :] = t0
                qhi[pl.ds(dest, 18, stride=2), :] = t1
                qlo[pl.ds(dest + 1, 18, stride=2), :] = jnp.where(lane18 < 64, r1, r2)
                qhi[pl.ds(dest + 1, 18, stride=2), :] = r2
        normed = layer_norm(tokens(qlo, qhi, rwin * TOK, TOK), g1[...]).astype(BF16)
        query = dot(normed, wqkv[:, :CH]) * (HD ** (-0.5) * LOG2E)
        for zwin in range(2):
            part = query[zwin * HALF : (zwin + 1) * HALF]
            for h in range(HEADS):
                stack[pl.ds(h * HALF, HALF), :] = jnp.where(head_of == h, part, 0.0)
            qst[rwin, zwin] = stack[...].astype(BF16)

    def tokens(low, high, start, size):
        return jnp.concatenate([low[start : start + size, :], high[start : start + size, : CH - 128]], axis=1)

    def attend(rwin, ew):
        tile = xin[ew, 6 * rwin : 6 * rwin + 6].astype(F32)
        frow[rwin * 432 : rwin * 432 + 432, :] = tile.reshape(432, 128)
        for zwin in range(2):
            for lev in range(2):
                base = rwin * 432 + LEVEL[zwin][lev]
                t0 = frow[pl.ds(base, 36, stride=12), :]
                t1 = frow[pl.ds(base + 4, 36, stride=12), :]
                t2 = frow[pl.ds(base + 8, 36, stride=12), :]
                r1 = pltpu.roll(t1, 64, 1)
                r2 = pltpu.roll(t2, 64, 1)
                dest = (rwin * 2 + zwin) * TOK + 72 * lev
                xlo[pl.ds(dest, 36, stride=2), :] = t0
                xhi[pl.ds(dest, 36, stride=2), :] = t1
                xlo[pl.ds(dest + 1, 36, stride=2), :] = jnp.where(lane36 < 64, r1, r2)
                xhi[pl.ds(dest + 1, 36, stride=2), :] = r2
        normed = layer_norm(tokens(xlo, xhi, rwin * 2 * TOK, 2 * TOK), g1[...]).astype(BF16)
        kv = dot(normed, wqkv[:, CH:]).astype(BF16)
        for zwin in range(2):
            mine = kv[zwin * TOK : (zwin + 1) * TOK]
            scores = dot_nt(qst[rwin, zwin], mine[:, :CH])
            brow = pl.ds(pl.multiple_of(((zwin * 2 + 1 - ew) * 2 + rwin) * 432, 8), 432)
            scores = scores + jnp.concatenate([blo[brow, :], bhi[brow, :][:, :16]], axis=1)
            top = jnp.max(scores, axis=-1, keepdims=True)
            probs = jnp.exp2(scores - top)
            total = jnp.sum(probs, axis=-1, keepdims=True)
            heads = dot(probs.astype(BF16), mine[:, CH:])
            mixed, norm = heads[:HALF], jnp.broadcast_to(total[:HALF], (HALF, CH))
            for h in range(1, HEADS):
                mixed = jnp.where(head_of == h, heads[h * HALF : (h + 1) * HALF], mixed)
                norm = jnp.where(head_of == h, total[h * HALF : (h + 1) * HALF], norm)
            mixs[rwin, zwin * HALF : (zwin + 1) * HALF, :] = mixed / norm

    def finish(rwins, ew):
        first, size = rwins[0] * TOK, len(rwins) * TOK
        mixed = jnp.concatenate([mixs[rwin] for rwin in rwins], axis=0)
        attn = dot(mixed.astype(BF16), wproj[...]).astype(BF16).astype(F32)
        resid = (tokens(qlo, qhi, first, size) + attn).astype(BF16).astype(F32)
        normed = layer_norm(resid, g2[...]).astype(BF16)
        hidden = jax.nn.gelu(dot(normed, w1[...])).astype(BF16)
        result = resid + dot_nt(hidden, w2t[...])
        rlo[first : first + size, :] = result[:, :128]
        rhi[first : first + size, : CH - 128] = result[:, 128:]
        columns = pl.ds(9 * ew, 9)
        for rwin in rwins:
            for zwin in range(2):
                for lev in range(2):
                    base = rwin * TOK + zwin * HALF + 36 * lev
                    even_lo = rlo[pl.ds(base, 18, stride=2), :]
                    even_hi = rhi[pl.ds(base, 18, stride=2), :]
                    odd_lo = pltpu.roll(rlo[pl.ds(base + 1, 18, stride=2), :], 64, 1)
                    odd_hi = pltpu.roll(rhi[pl.ds(base + 1, 18, stride=2), :], 64, 1)
                    dest = rwin * 216 + LEVEL[zwin][lev]
                    orow[pl.ds(dest, 18, stride=12), :] = even_lo
                    orow[pl.ds(dest + 4, 18, stride=12), :] = jnp.where(lane18 < 64, even_hi, odd_lo)
                    orow[pl.ds(dest + 8, 18, stride=12), :] = jnp.where(lane18 < 64, odd_lo, odd_hi)
            tile = orow[rwin * 216 : rwin * 216 + 216, :].reshape(6, 9, 4, 128).astype(BF16)
            if rwin == 0:
                out[3:9, columns] = tile
            else:
                out[9:12, columns] = tile[:3]
                back[:, columns] = tile[3:]
                give_back(ew).start()

    def arrive(which, rwin, ew):
        for side in range(2):

            @pl.when(ew == side)
            def _(side=side):
                for i in which[side][rwin]:
                    halo[i].wait_recv()

    early = jnp.where(across, 1, 0)
    late = 1 - early
    for rwin in range(2):
        arrive(query_needs, rwin, early)
        queries(rwin, early)
        arrive(key_needs, rwin, early)
        attend(rwin, early)
    finish((0, 1), early)
    for rwin in (1, 0):
        arrive(query_needs, rwin, late)
        queries(rwin, late)
    pl.when(across)(westward)
    for rwin in (1, 0):
        arrive(key_needs, rwin, late)
        attend(rwin, late)
        finish((rwin,), late)
    for copy in halo:
        copy.wait_send()
    for ew in range(2):
        give_back(ew).wait()


def shards(field_in, g1, wqkv, wproj, bias, g2, w1, w2):
    lons, lats = lax.axis_size("lon"), lax.axis_size("lat")
    x = field_in.reshape(4, 12, 18, 128).transpose(1, 2, 0, 3)
    flat = bias.transpose(0, 2, 1, 3).reshape(12, 2, 20736)
    hbm = pl.BlockSpec(memory_space=pltpu.MemorySpace.HBM)
    result = pl.pallas_call(
        functools.partial(block_kernel, lons, lats),
        out_shape=pltpu.VMEM((12, 18, 4, 128), BF16),
        in_specs=[hbm] * 8,
        out_specs=pl.BlockSpec(memory_space=pltpu.VMEM),
        scratch_shapes=[
            pltpu.VMEM((2, 12, 18, 4, 128), BF16),
            pltpu.VMEM((12, 2, 20736), F32),
            pltpu.VMEM((3888, 128), F32),
            pltpu.VMEM((3456, 128), F32),
            pltpu.VMEM((3456, 128), F32),
            pltpu.VMEM((432, 128), F32),
            pltpu.VMEM((288, 128), F32),
            pltpu.VMEM((288, 128), F32),
            pltpu.VMEM((432, CH), F32),
            pltpu.VMEM((2, 2, 432, CH), BF16),
            pltpu.VMEM((864, 128), F32),
            pltpu.VMEM((576, 128), F32),
            pltpu.VMEM((576, 128), F32),
            pltpu.VMEM((2, TOK, CH), F32),
            pltpu.VMEM((2 * TOK, 128), F32),
            pltpu.VMEM((2 * TOK, 128), F32),
            pltpu.VMEM((432, 128), F32),
            pltpu.VMEM((3, 18, 4, 128), BF16),
            pltpu.VMEM((CH,), F32),
            pltpu.VMEM((CH,), F32),
            pltpu.VMEM((CH, 3 * CH), BF16),
            pltpu.VMEM((CH, CH), BF16),
            pltpu.VMEM((CH, 768), BF16),
            pltpu.VMEM((CH, 768), BF16),
            pltpu.SemaphoreType.DMA((7,)),
            pltpu.SemaphoreType.DMA((2,)),
            pltpu.SemaphoreType.DMA((10,)),
            pltpu.SemaphoreType.DMA((10,)),
            pltpu.SemaphoreType.REGULAR((3,)),
        ],
        compiler_params=pltpu.CompilerParams(
            collective_id=0, has_side_effects=True, vmem_limit_bytes=60 * 1024 * 1024
        ),
        name="swin_block",
    )(x, g1, wqkv, wproj, flat, g2, w1, w2.T)
    return result.transpose(2, 0, 1, 3).reshape(4, 12, 12 * CH)


def solution(mesh):
    in_specs = (P(None, "lat", "lon"), P(), P(), P(), P("lat", None, None, None), P(), P(), P())
    return jax.shard_map(
        shards, mesh=mesh, in_specs=in_specs, out_specs=P(None, "lat", "lon"), check_vma=False
    )
```

```python
import functools

import jax
import jax.numpy as jnp
from jax import lax
from jax.experimental import pallas as pl
from jax.experimental.pallas import tpu as pltpu
from jax.sharding import PartitionSpec as P

MESH = pl.DeviceIdType.MESH
BF16 = jnp.bfloat16
F32 = jnp.float32
CH = 192
HEADS = 6
HD = CH // HEADS
TOK = 144
HALF = TOK // 2
LEVEL = ((1, 2), (3, 0))
NEG = -1000000000.0
LOG2E = 1.4426950408889634


def dot_nt(a, b):
    return lax.dot_general(a, b, (((1,), (1,)), ((), ())), preferred_element_type=F32)


def dot(a, b):
    return jnp.dot(a, b, preferred_element_type=F32)


def row_mean(values):
    mean = dot(values.astype(BF16), jnp.ones((CH, 128), BF16)) * (1.0 / CH)
    return jnp.concatenate([mean, mean[:, : CH - 128]], axis=1)


def layer_norm(values, gain):
    center = values - row_mean(values)
    spread = row_mean(center * center)
    return center * lax.rsqrt(spread + 1e-05) * gain


def block_kernel(
    lons, lats,
    x_hbm, g1_hbm, wqkv_hbm, wproj_hbm, bias_hbm, g2_hbm, w1_hbm, w2t_hbm,
    out,
    xin, raw, lin, blo, bhi, fq, qlo, qhi, stack, qst, frow, xlo, xhi, mixs, rlo, rhi, orow, back,
    g1, g2, wqkv, wproj, w1, w2t,
    load_sem, own_sem, send_sem, recv_sem, ready,
):
    lon = lax.axis_index("lon")
    lat = lax.axis_index("lat")
    east = lax.rem(lon + 1, lons)
    west = lax.rem(lon + lons - 1, lons)
    south = lax.rem(lat + 1, lats)
    north = lax.rem(lat + lats - 1, lats)

    barrier = pltpu.get_barrier_semaphore()
    for a, b in ((west, lat), (lon, north), (west, south), (west, north)):
        pl.semaphore_signal(barrier, inc=1, device_id={"lon": a, "lat": b}, device_id_type=MESH)

    loads = [
        pltpu.make_async_copy(src, dst, load_sem.at[i])
        for i, (src, dst) in enumerate(
            (
                (bias_hbm, raw), (g1_hbm, g1), (wqkv_hbm, wqkv), (wproj_hbm, wproj),
                (g2_hbm, g2), (w1_hbm, w1), (w2t_hbm, w2t),
            )
        )
    ]
    own = [
        pltpu.make_async_copy(x_hbm.at[3:12, 0:9], xin.at[0, 0:9, 9:18], own_sem.at[0]),
        pltpu.make_async_copy(x_hbm.at[3:12, 9:18], xin.at[1, 0:9, 0:9], own_sem.at[1]),
    ]
    for copy in own + loads:
        copy.start()

    def remote(i, src, dst, a, b):
        return pltpu.make_async_remote_copy(
            src_ref=src, dst_ref=dst, send_sem=send_sem.at[i], recv_sem=recv_sem.at[i],
            device_id={"lon": a, "lat": b}, device_id_type=MESH,
        )

    halo = [
        remote(0, x_hbm.at[9:12, 9:18], xin.at[0, 6:9, 0:9], east, lat),
        remote(1, x_hbm.at[0:3, 9:18], xin.at[0, 9:12, 0:9], east, north),
        remote(2, x_hbm.at[3:9, 9:18], xin.at[0, 0:6, 0:9], east, lat),
        remote(3, x_hbm.at[3:9, 0:9], xin.at[1, 0:6, 9:18], west, lat),
        remote(4, x_hbm.at[9:12, 0:9], xin.at[1, 6:9, 9:18], west, lat),
        remote(5, x_hbm.at[0:3, 0:9], xin.at[1, 9:12, 9:18], west, north),
        remote(6, x_hbm.at[0:3, 9:18], xin.at[1, 9:12, 0:9], lon, north),
        remote(7, x_hbm.at[0:3, 0:9], xin.at[0, 9:12, 9:18], lon, north),
    ]
    query_needs = (((), (7,)), ((), (6,)))
    key_needs = (((2,), (0, 1)), ((3,), (4, 5)))

    def give_back(ew):
        columns = pl.ds(9 * ew, 9)
        return remote(8 + ew, back.at[:, columns], out.at[0:3, columns], lon, south)


    pl.semaphore_wait(barrier, 4)
    for i, (a, b) in enumerate(((east, lat), (east, south), (lon, south))):
        pl.semaphore_signal(ready.at[i], inc=1, device_id={"lon": a, "lat": b}, device_id_type=MESH)
    for i in (1, 0, 2):
        halo[i].start()

    def westward():
        pl.semaphore_wait(ready.at[0], 1)
        pl.semaphore_wait(ready.at[1], 1)
        for i in (3, 4, 5):
            halo[i].start()

    loads[0].wait()

    def linear(rh, carry):
        base = pl.multiple_of(rh * 324, 4)
        for t in range(162):
            lin[pl.ds(base + 2 * t, 2), :] = raw[rh, :, 128 * t : 128 * t + 128]
        return carry

    lax.fori_loop(0, 12, linear, 0)

    lanes = lax.broadcasted_iota(jnp.int32, (72, 128), 1)
    place = lax.broadcasted_iota(jnp.int32, (72, 128), 0)
    step = lax.rem(place, 6)
    level_q = step // 3
    last = jnp.where(lat == lats - 1, NEG, 0.0).astype(F32)

    def key_level(key):
        return key // 72

    def key_edge(key):
        return lax.rem(key // 12, 6) // 3

    edge_rows = place >= 36

    def penalty(key, odd, zwin):
        row_q = lax.rem(2 * step + odd, 6) // 3
        pen = jnp.where(jnp.logical_and(edge_rows, row_q != key_edge(key)), last, 0.0)
        if zwin:
            pen = pen + jnp.where(level_q != key_level(key), NEG, 0.0)
        return pen

    for zwin in range(2):
        for odd in range(2):
            pen_lo = penalty(lanes, odd, zwin)
            pen_hi = penalty(lanes + 128, odd, zwin)
            for wc in range(12):
                c = 12 * odd + wc
                start = (9 * (c // 8) + c % 8) * 2 + zwin
                this = lin[pl.ds(start, 72, stride=54), :]
                following = lin[pl.ds(start + 2, 72, stride=54), :]
                turn = 16 * (c % 8)
                if turn:
                    this = pltpu.roll(this, 128 - turn, 1)
                    following = pltpu.roll(following, 128 - turn, 1)
                low = jnp.where(lanes < 128 - turn, this, following)
                dest = (zwin * 2 + wc // 6) * 864 + 6 * odd + wc % 6
                blo[pl.ds(dest, 72, stride=12), :] = low * LOG2E + pen_lo
                bhi[pl.ds(dest, 72, stride=12), :] = jnp.where(lanes < TOK - 128, following * LOG2E + pen_hi, NEG)

    pl.semaphore_wait(ready.at[2], 1)
    for i in (6, 7):
        halo[i].start()
    across = lax.rem(lon, 16) == 0

    @pl.when(jnp.logical_not(across))
    def _():
        westward()

    for copy in loads[1:]:
        copy.wait()
    for copy in own:
        copy.wait()

    lane36 = lax.broadcasted_iota(jnp.int32, (36, 128), 1)
    lane18 = lax.broadcasted_iota(jnp.int32, (18, 128), 1)

    head_of = lax.broadcasted_iota(jnp.int32, (HALF, CH), 1) // HD

    def queries(rwin, ew):
        own_tiles = pl.ds(9 - 9 * ew, 9)
        tile = xin[ew, 6 * rwin : 6 * rwin + 6, own_tiles].astype(F32)
        fq[rwin * 216 : rwin * 216 + 216, :] = tile.reshape(216, 128)
        for zwin in range(2):
            for lev in range(2):
                base = rwin * 216 + LEVEL[zwin][lev]
                t0 = fq[pl.ds(base, 18, stride=12), :]
                t1 = fq[pl.ds(base + 4, 18, stride=12), :]
                t2 = fq[pl.ds(base + 8, 18, stride=12), :]
                r1 = pltpu.roll(t1, 64, 1)
                r2 = pltpu.roll(t2, 64, 1)
                dest = rwin * TOK + zwin * HALF + 36 * lev
                qlo[pl.ds(dest, 18, stride=2), :] = t0
                qhi[pl.ds(dest, 18, stride=2), :] = t1
                qlo[pl.ds(dest + 1, 18, stride=2), :] = jnp.where(lane18 < 64, r1, r2)
                qhi[pl.ds(dest + 1, 18, stride=2), :] = r2
        normed = layer_norm(tokens(qlo, qhi, rwin * TOK, TOK), g1[...]).astype(BF16)
        query = dot(normed, wqkv[:, :CH]) * (HD ** (-0.5) * LOG2E)
        for zwin in range(2):
            part = query[zwin * HALF : (zwin + 1) * HALF]
            for h in range(HEADS):
                stack[pl.ds(h * HALF, HALF), :] = jnp.where(head_of == h, part, 0.0)
            qst[rwin, zwin] = stack[...].astype(BF16)

    def tokens(low, high, start, size):
        return jnp.concatenate([low[start : start + size, :], high[start : start + size, : CH - 128]], axis=1)

    def attend(rwin, ew):
        tile = xin[ew, 6 * rwin : 6 * rwin + 6].astype(F32)
        frow[rwin * 432 : rwin * 432 + 432, :] = tile.reshape(432, 128)
        for zwin in range(2):
            for lev in range(2):
                base = rwin * 432 + LEVEL[zwin][lev]
                t0 = frow[pl.ds(base, 36, stride=12), :]
                t1 = frow[pl.ds(base + 4, 36, stride=12), :]
                t2 = frow[pl.ds(base + 8, 36, stride=12), :]
                r1 = pltpu.roll(t1, 64, 1)
                r2 = pltpu.roll(t2, 64, 1)
                dest = (rwin * 2 + zwin) * TOK + 72 * lev
                xlo[pl.ds(dest, 36, stride=2), :] = t0
                xhi[pl.ds(dest, 36, stride=2), :] = t1
                xlo[pl.ds(dest + 1, 36, stride=2), :] = jnp.where(lane36 < 64, r1, r2)
                xhi[pl.ds(dest + 1, 36, stride=2), :] = r2
        normed = layer_norm(tokens(xlo, xhi, rwin * 2 * TOK, 2 * TOK), g1[...]).astype(BF16)
        kv = dot(normed, wqkv[:, CH:]).astype(BF16)
        blank = jnp.zeros((256 - TOK, 2 * CH), BF16)
        for zwin in range(2):
            mine = jnp.concatenate([kv[zwin * TOK : (zwin + 1) * TOK], blank], axis=0)
            scores = dot_nt(qst[rwin, zwin], mine[:, :CH])
            brow = pl.ds(pl.multiple_of(((zwin * 2 + 1 - ew) * 2 + rwin) * 432, 8), 432)
            scores = scores + jnp.concatenate([blo[brow, :], bhi[brow, :]], axis=1)
            top = jnp.max(scores, axis=-1, keepdims=True)
            probs = jnp.exp2(scores - top)
            total = jnp.sum(probs, axis=-1, keepdims=True)
            heads = dot(probs.astype(BF16), mine[:, CH:])
            mixed, norm = heads[:HALF], jnp.broadcast_to(total[:HALF], (HALF, CH))
            for h in range(1, HEADS):
                mixed = jnp.where(head_of == h, heads[h * HALF : (h + 1) * HALF], mixed)
                norm = jnp.where(head_of == h, total[h * HALF : (h + 1) * HALF], norm)
            mixs[rwin, zwin * HALF : (zwin + 1) * HALF, :] = mixed / norm

    def finish(rwins, ew):
        first, size = rwins[0] * TOK, len(rwins) * TOK
        mixed = jnp.concatenate([mixs[rwin] for rwin in rwins], axis=0)
        attn = dot(mixed.astype(BF16), wproj[...]).astype(BF16).astype(F32)
        resid = (tokens(qlo, qhi, first, size) + attn).astype(BF16).astype(F32)
        normed = layer_norm(resid, g2[...]).astype(BF16)
        hidden = jax.nn.gelu(dot(normed, w1[...])).astype(BF16)
        result = resid + dot_nt(hidden, w2t[...])
        rlo[first : first + size, :] = result[:, :128]
        rhi[first : first + size, : CH - 128] = result[:, 128:]
        columns = pl.ds(9 * ew, 9)
        for rwin in rwins:
            for zwin in range(2):
                for lev in range(2):
                    base = rwin * TOK + zwin * HALF + 36 * lev
                    even_lo = rlo[pl.ds(base, 18, stride=2), :]
                    even_hi = rhi[pl.ds(base, 18, stride=2), :]
                    odd_lo = pltpu.roll(rlo[pl.ds(base + 1, 18, stride=2), :], 64, 1)
                    odd_hi = pltpu.roll(rhi[pl.ds(base + 1, 18, stride=2), :], 64, 1)
                    dest = rwin * 216 + LEVEL[zwin][lev]
                    orow[pl.ds(dest, 18, stride=12), :] = even_lo
                    orow[pl.ds(dest + 4, 18, stride=12), :] = jnp.where(lane18 < 64, even_hi, odd_lo)
                    orow[pl.ds(dest + 8, 18, stride=12), :] = jnp.where(lane18 < 64, odd_lo, odd_hi)
            tile = orow[rwin * 216 : rwin * 216 + 216, :].reshape(6, 9, 4, 128).astype(BF16)
            if rwin == 0:
                out[3:9, columns] = tile
            else:
                out[9:12, columns] = tile[:3]
                back[:, columns] = tile[3:]
                give_back(ew).start()

    def arrive(which, rwin, ew):
        for side in range(2):

            @pl.when(ew == side)
            def _(side=side):
                for i in which[side][rwin]:
                    halo[i].wait_recv()

    early = jnp.where(across, 1, 0)
    late = 1 - early
    for rwin in range(2):
        arrive(query_needs, rwin, early)
        queries(rwin, early)
        arrive(key_needs, rwin, early)
        attend(rwin, early)
    finish((0, 1), early)
    for rwin in (1, 0):
        arrive(query_needs, rwin, late)
        queries(rwin, late)
    pl.when(across)(westward)
    for rwin in (1, 0):
        arrive(key_needs, rwin, late)
        attend(rwin, late)
        finish((rwin,), late)
    for copy in halo:
        copy.wait_send()
    for ew in range(2):
        give_back(ew).wait()


def shards(field_in, g1, wqkv, wproj, bias, g2, w1, w2):
    lons, lats = lax.axis_size("lon"), lax.axis_size("lat")
    x = field_in.reshape(4, 12, 18, 128).transpose(1, 2, 0, 3)
    flat = bias.transpose(0, 2, 1, 3).reshape(12, 2, 20736)
    hbm = pl.BlockSpec(memory_space=pltpu.MemorySpace.HBM)
    result = pl.pallas_call(
        functools.partial(block_kernel, lons, lats),
        out_shape=pltpu.VMEM((12, 18, 4, 128), BF16),
        in_specs=[hbm] * 8,
        out_specs=pl.BlockSpec(memory_space=pltpu.VMEM),
        scratch_shapes=[
            pltpu.VMEM((2, 12, 18, 4, 128), BF16),
            pltpu.VMEM((12, 2, 20736), F32),
            pltpu.VMEM((3888, 128), F32),
            pltpu.VMEM((3456, 128), F32),
            pltpu.VMEM((3456, 128), F32),
            pltpu.VMEM((432, 128), F32),
            pltpu.VMEM((288, 128), F32),
            pltpu.VMEM((288, 128), F32),
            pltpu.VMEM((432, CH), F32),
            pltpu.VMEM((2, 2, 432, CH), BF16),
            pltpu.VMEM((864, 128), F32),
            pltpu.VMEM((576, 128), F32),
            pltpu.VMEM((576, 128), F32),
            pltpu.VMEM((2, TOK, CH), F32),
            pltpu.VMEM((2 * TOK, 128), F32),
            pltpu.VMEM((2 * TOK, 128), F32),
            pltpu.VMEM((432, 128), F32),
            pltpu.VMEM((3, 18, 4, 128), BF16),
            pltpu.VMEM((CH,), F32),
            pltpu.VMEM((CH,), F32),
            pltpu.VMEM((CH, 3 * CH), BF16),
            pltpu.VMEM((CH, CH), BF16),
            pltpu.VMEM((CH, 768), BF16),
            pltpu.VMEM((CH, 768), BF16),
            pltpu.SemaphoreType.DMA((7,)),
            pltpu.SemaphoreType.DMA((2,)),
            pltpu.SemaphoreType.DMA((10,)),
            pltpu.SemaphoreType.DMA((10,)),
            pltpu.SemaphoreType.REGULAR((3,)),
        ],
        compiler_params=pltpu.CompilerParams(
            collective_id=0, has_side_effects=True, vmem_limit_bytes=60 * 1024 * 1024
        ),
        name="swin_block",
    )(x, g1, wqkv, wproj, flat, g2, w1, w2.T)
    return result.transpose(2, 0, 1, 3).reshape(4, 12, 12 * CH)


def solution(mesh):
    in_specs = (P(None, "lat", "lon"), P(), P(), P(), P("lat", None, None, None), P(), P(), P())
    return jax.shard_map(
        shards, mesh=mesh, in_specs=in_specs, out_specs=P(None, "lat", "lon"), check_vma=False
    )
```

```python
import functools

import jax
import jax.numpy as jnp
from jax import lax
from jax.experimental import pallas as pl
from jax.experimental.pallas import tpu as pltpu
from jax.sharding import PartitionSpec as P

MESH = pl.DeviceIdType.MESH
BF16 = jnp.bfloat16
F32 = jnp.float32
CH = 192
HEADS = 6
HD = CH // HEADS
TOK = 144
HALF = TOK // 2
LEVEL = ((1, 2), (3, 0))
NEG = -1000000000.0
LOG2E = 1.4426950408889634


def dot_nt(a, b):
    return lax.dot_general(a, b, (((1,), (1,)), ((), ())), preferred_element_type=F32)


def dot(a, b):
    return jnp.dot(a, b, preferred_element_type=F32)


def row_mean(values):
    mean = dot(values.astype(BF16), jnp.ones((CH, 128), BF16)) * (1.0 / CH)
    return jnp.concatenate([mean, mean[:, : CH - 128]], axis=1)


def layer_norm(values, gain):
    center = values - row_mean(values)
    spread = row_mean(center * center)
    return center * lax.rsqrt(spread + 1e-05) * gain


def block_kernel(
    lons, lats,
    x_hbm, g1_hbm, wqkv_hbm, wproj_hbm, bias_hbm, g2_hbm, w1_hbm, w2t_hbm,
    out,
    xin, raw, lin, blo, bhi, fq, qlo, qhi, stack, qst, frow, xlo, xhi, mixs, rlo, rhi, orow, back,
    g1, g2, wqkv, wproj, w1, w2t,
    load_sem, own_sem, send_sem, recv_sem, ready,
):
    lon = lax.axis_index("lon")
    lat = lax.axis_index("lat")
    east = lax.rem(lon + 1, lons)
    west = lax.rem(lon + lons - 1, lons)
    south = lax.rem(lat + 1, lats)
    north = lax.rem(lat + lats - 1, lats)

    barrier = pltpu.get_barrier_semaphore()
    for a, b in ((west, lat), (lon, north), (west, south), (west, north)):
        pl.semaphore_signal(barrier, inc=1, device_id={"lon": a, "lat": b}, device_id_type=MESH)

    loads = [
        pltpu.make_async_copy(src, dst, load_sem.at[i])
        for i, (src, dst) in enumerate(
            (
                (bias_hbm, raw), (g1_hbm, g1), (wqkv_hbm, wqkv), (wproj_hbm, wproj),
                (g2_hbm, g2), (w1_hbm, w1), (w2t_hbm, w2t),
            )
        )
    ]
    own = [
        pltpu.make_async_copy(x_hbm.at[3:12, 0:9], xin.at[0, 0:9, 9:18], own_sem.at[0]),
        pltpu.make_async_copy(x_hbm.at[3:12, 9:18], xin.at[1, 0:9, 0:9], own_sem.at[1]),
    ]
    for copy in own + loads:
        copy.start()

    def remote(i, src, dst, a, b):
        return pltpu.make_async_remote_copy(
            src_ref=src, dst_ref=dst, send_sem=send_sem.at[i], recv_sem=recv_sem.at[i],
            device_id={"lon": a, "lat": b}, device_id_type=MESH,
        )

    halo = [
        remote(0, x_hbm.at[9:12, 9:18], xin.at[0, 6:9, 0:9], east, lat),
        remote(1, x_hbm.at[0:3, 9:18], xin.at[0, 9:12, 0:9], east, north),
        remote(2, x_hbm.at[3:9, 9:18], xin.at[0, 0:6, 0:9], east, lat),
        remote(3, x_hbm.at[3:9, 0:9], xin.at[1, 0:6, 9:18], west, lat),
        remote(4, x_hbm.at[9:12, 0:9], xin.at[1, 6:9, 9:18], west, lat),
        remote(5, x_hbm.at[0:3, 0:9], xin.at[1, 9:12, 9:18], west, north),
        remote(6, x_hbm.at[0:3, 9:18], xin.at[1, 9:12, 0:9], lon, north),
        remote(7, x_hbm.at[0:3, 0:9], xin.at[0, 9:12, 9:18], lon, north),
    ]
    query_needs = (((), (7,)), ((), (6,)))
    key_needs = (((2,), (0, 1)), ((3,), (4, 5)))

    def give_back(ew):
        columns = pl.ds(9 * ew, 9)
        return remote(8 + ew, back.at[:, columns], out.at[0:3, columns], lon, south)


    pl.semaphore_wait(barrier, 4)
    for i, (a, b) in enumerate(((east, lat), (east, south), (lon, south))):
        pl.semaphore_signal(ready.at[i], inc=1, device_id={"lon": a, "lat": b}, device_id_type=MESH)
    for i in (1, 0, 2):
        halo[i].start()

    def westward():
        pl.semaphore_wait(ready.at[0], 1)
        for i in (4, 3):
            halo[i].start()
        pl.semaphore_wait(ready.at[1], 1)
        halo[5].start()

    loads[0].wait()

    def linear(rh, carry):
        base = pl.multiple_of(rh * 324, 4)
        for t in range(162):
            lin[pl.ds(base + 2 * t, 2), :] = raw[rh, :, 128 * t : 128 * t + 128]
        return carry

    lax.fori_loop(0, 12, linear, 0)

    lanes = lax.broadcasted_iota(jnp.int32, (72, 128), 1)
    place = lax.broadcasted_iota(jnp.int32, (72, 128), 0)
    step = lax.rem(place, 6)
    level_q = step // 3
    last = jnp.where(lat == lats - 1, NEG, 0.0).astype(F32)

    def key_level(key):
        return key // 72

    def key_edge(key):
        return lax.rem(key // 12, 6) // 3

    edge_rows = place >= 36

    def penalty(key, odd, zwin):
        row_q = lax.rem(2 * step + odd, 6) // 3
        pen = jnp.where(jnp.logical_and(edge_rows, row_q != key_edge(key)), last, 0.0)
        if zwin:
            pen = pen + jnp.where(level_q != key_level(key), NEG, 0.0)
        return pen

    for zwin in range(2):
        for odd in range(2):
            pen_lo = penalty(lanes, odd, zwin)
            pen_hi = penalty(lanes + 128, odd, zwin)
            for wc in range(12):
                c = 12 * odd + wc
                start = (9 * (c // 8) + c % 8) * 2 + zwin
                this = lin[pl.ds(start, 72, stride=54), :]
                following = lin[pl.ds(start + 2, 72, stride=54), :]
                turn = 16 * (c % 8)
                if turn:
                    this = pltpu.roll(this, 128 - turn, 1)
                    following = pltpu.roll(following, 128 - turn, 1)
                low = jnp.where(lanes < 128 - turn, this, following)
                dest = (zwin * 2 + wc // 6) * 864 + 6 * odd + wc % 6
                blo[pl.ds(dest, 72, stride=12), :] = low * LOG2E + pen_lo
                bhi[pl.ds(dest, 72, stride=12), :] = jnp.where(lanes < TOK - 128, following * LOG2E + pen_hi, NEG)

    pl.semaphore_wait(ready.at[2], 1)
    for i in (6, 7):
        halo[i].start()
    across = lax.rem(lon, 16) == 0

    @pl.when(jnp.logical_not(across))
    def _():
        westward()

    for copy in loads[1:]:
        copy.wait()
    for copy in own:
        copy.wait()

    lane36 = lax.broadcasted_iota(jnp.int32, (36, 128), 1)
    lane18 = lax.broadcasted_iota(jnp.int32, (18, 128), 1)

    head_of = lax.broadcasted_iota(jnp.int32, (HALF, CH), 1) // HD

    def queries(rwin, ew):
        own_tiles = pl.ds(9 - 9 * ew, 9)
        tile = xin[ew, 6 * rwin : 6 * rwin + 6, own_tiles].astype(F32)
        fq[rwin * 216 : rwin * 216 + 216, :] = tile.reshape(216, 128)
        for zwin in range(2):
            for lev in range(2):
                base = rwin * 216 + LEVEL[zwin][lev]
                t0 = fq[pl.ds(base, 18, stride=12), :]
                t1 = fq[pl.ds(base + 4, 18, stride=12), :]
                t2 = fq[pl.ds(base + 8, 18, stride=12), :]
                r1 = pltpu.roll(t1, 64, 1)
                r2 = pltpu.roll(t2, 64, 1)
                dest = rwin * TOK + zwin * HALF + 36 * lev
                qlo[pl.ds(dest, 18, stride=2), :] = t0
                qhi[pl.ds(dest, 18, stride=2), :] = t1
                qlo[pl.ds(dest + 1, 18, stride=2), :] = jnp.where(lane18 < 64, r1, r2)
                qhi[pl.ds(dest + 1, 18, stride=2), :] = r2
        normed = layer_norm(tokens(qlo, qhi, rwin * TOK, TOK), g1[...]).astype(BF16)
        query = dot(normed, wqkv[:, :CH]) * (HD ** (-0.5) * LOG2E)
        for zwin in range(2):
            part = query[zwin * HALF : (zwin + 1) * HALF]
            for h in range(HEADS):
                stack[pl.ds(h * HALF, HALF), :] = jnp.where(head_of == h, part, 0.0)
            qst[rwin, zwin] = stack[...].astype(BF16)

    def tokens(low, high, start, size):
        return jnp.concatenate([low[start : start + size, :], high[start : start + size, : CH - 128]], axis=1)

    def attend(rwin, ew):
        tile = xin[ew, 6 * rwin : 6 * rwin + 6].astype(F32)
        frow[rwin * 432 : rwin * 432 + 432, :] = tile.reshape(432, 128)
        for zwin in range(2):
            for lev in range(2):
                base = rwin * 432 + LEVEL[zwin][lev]
                t0 = frow[pl.ds(base, 36, stride=12), :]
                t1 = frow[pl.ds(base + 4, 36, stride=12), :]
                t2 = frow[pl.ds(base + 8, 36, stride=12), :]
                r1 = pltpu.roll(t1, 64, 1)
                r2 = pltpu.roll(t2, 64, 1)
                dest = (rwin * 2 + zwin) * TOK + 72 * lev
                xlo[pl.ds(dest, 36, stride=2), :] = t0
                xhi[pl.ds(dest, 36, stride=2), :] = t1
                xlo[pl.ds(dest + 1, 36, stride=2), :] = jnp.where(lane36 < 64, r1, r2)
                xhi[pl.ds(dest + 1, 36, stride=2), :] = r2
        normed = layer_norm(tokens(xlo, xhi, rwin * 2 * TOK, 2 * TOK), g1[...]).astype(BF16)
        kv = dot(normed, wqkv[:, CH:]).astype(BF16)
        blank = jnp.zeros((256 - TOK, 2 * CH), BF16)
        for zwin in range(2):
            mine = jnp.concatenate([kv[zwin * TOK : (zwin + 1) * TOK], blank], axis=0)
            scores = dot_nt(qst[rwin, zwin], mine[:, :CH])
            brow = pl.ds(pl.multiple_of(((zwin * 2 + 1 - ew) * 2 + rwin) * 432, 8), 432)
            scores = scores + jnp.concatenate([blo[brow, :], bhi[brow, :]], axis=1)
            top = jnp.max(scores, axis=-1, keepdims=True)
            probs = jnp.exp2(scores - top)
            total = jnp.sum(probs, axis=-1, keepdims=True)
            heads = dot(probs.astype(BF16), mine[:, CH:])
            mixed, norm = heads[:HALF], jnp.broadcast_to(total[:HALF], (HALF, CH))
            for h in range(1, HEADS):
                mixed = jnp.where(head_of == h, heads[h * HALF : (h + 1) * HALF], mixed)
                norm = jnp.where(head_of == h, total[h * HALF : (h + 1) * HALF], norm)
            mixs[rwin, zwin * HALF : (zwin + 1) * HALF, :] = mixed / norm

    def finish(rwins, ew):
        first, size = rwins[0] * TOK, len(rwins) * TOK
        mixed = jnp.concatenate([mixs[rwin] for rwin in rwins], axis=0)
        attn = dot(mixed.astype(BF16), wproj[...]).astype(BF16).astype(F32)
        resid = (tokens(qlo, qhi, first, size) + attn).astype(BF16).astype(F32)
        normed = layer_norm(resid, g2[...]).astype(BF16)
        hidden = jax.nn.gelu(dot(normed, w1[...])).astype(BF16)
        result = resid + dot_nt(hidden, w2t[...])
        rlo[first : first + size, :] = result[:, :128]
        rhi[first : first + size, : CH - 128] = result[:, 128:]
        columns = pl.ds(9 * ew, 9)
        for rwin in rwins:
            for zwin in range(2):
                for lev in range(2):
                    base = rwin * TOK + zwin * HALF + 36 * lev
                    even_lo = rlo[pl.ds(base, 18, stride=2), :]
                    even_hi = rhi[pl.ds(base, 18, stride=2), :]
                    odd_lo = pltpu.roll(rlo[pl.ds(base + 1, 18, stride=2), :], 64, 1)
                    odd_hi = pltpu.roll(rhi[pl.ds(base + 1, 18, stride=2), :], 64, 1)
                    dest = rwin * 216 + LEVEL[zwin][lev]
                    orow[pl.ds(dest, 18, stride=12), :] = even_lo
                    orow[pl.ds(dest + 4, 18, stride=12), :] = jnp.where(lane18 < 64, even_hi, odd_lo)
                    orow[pl.ds(dest + 8, 18, stride=12), :] = jnp.where(lane18 < 64, odd_lo, odd_hi)
            tile = orow[rwin * 216 : rwin * 216 + 216, :].reshape(6, 9, 4, 128).astype(BF16)
            if rwin == 0:
                out[3:9, columns] = tile
            else:
                out[9:12, columns] = tile[:3]
                back[:, columns] = tile[3:]
                give_back(ew).start()

    def arrive(which, rwin, ew):
        for side in range(2):

            @pl.when(ew == side)
            def _(side=side):
                for i in which[side][rwin]:
                    halo[i].wait_recv()

    early = jnp.where(across, 1, 0)
    late = 1 - early
    for rwin in range(2):
        arrive(query_needs, rwin, early)
        queries(rwin, early)
        arrive(key_needs, rwin, early)
        attend(rwin, early)
    finish((0, 1), early)
    for rwin in (1, 0):
        arrive(query_needs, rwin, late)
        queries(rwin, late)
    pl.when(across)(westward)
    for rwin in (1, 0):
        arrive(key_needs, rwin, late)
        attend(rwin, late)
        finish((rwin,), late)
    for copy in halo:
        copy.wait_send()
    for ew in range(2):
        give_back(ew).wait()


def shards(field_in, g1, wqkv, wproj, bias, g2, w1, w2):
    lons, lats = lax.axis_size("lon"), lax.axis_size("lat")
    x = field_in.reshape(4, 12, 18, 128).transpose(1, 2, 0, 3)
    flat = bias.transpose(0, 2, 1, 3).reshape(12, 2, 20736)
    hbm = pl.BlockSpec(memory_space=pltpu.MemorySpace.HBM)
    result = pl.pallas_call(
        functools.partial(block_kernel, lons, lats),
        out_shape=pltpu.VMEM((12, 18, 4, 128), BF16),
        in_specs=[hbm] * 8,
        out_specs=pl.BlockSpec(memory_space=pltpu.VMEM),
        scratch_shapes=[
            pltpu.VMEM((2, 12, 18, 4, 128), BF16),
            pltpu.VMEM((12, 2, 20736), F32),
            pltpu.VMEM((3888, 128), F32),
            pltpu.VMEM((3456, 128), F32),
            pltpu.VMEM((3456, 128), F32),
            pltpu.VMEM((432, 128), F32),
            pltpu.VMEM((288, 128), F32),
            pltpu.VMEM((288, 128), F32),
            pltpu.VMEM((432, CH), F32),
            pltpu.VMEM((2, 2, 432, CH), BF16),
            pltpu.VMEM((864, 128), F32),
            pltpu.VMEM((576, 128), F32),
            pltpu.VMEM((576, 128), F32),
            pltpu.VMEM((2, TOK, CH), F32),
            pltpu.VMEM((2 * TOK, 128), F32),
            pltpu.VMEM((2 * TOK, 128), F32),
            pltpu.VMEM((432, 128), F32),
            pltpu.VMEM((3, 18, 4, 128), BF16),
            pltpu.VMEM((CH,), F32),
            pltpu.VMEM((CH,), F32),
            pltpu.VMEM((CH, 3 * CH), BF16),
            pltpu.VMEM((CH, CH), BF16),
            pltpu.VMEM((CH, 768), BF16),
            pltpu.VMEM((CH, 768), BF16),
            pltpu.SemaphoreType.DMA((7,)),
            pltpu.SemaphoreType.DMA((2,)),
            pltpu.SemaphoreType.DMA((10,)),
            pltpu.SemaphoreType.DMA((10,)),
            pltpu.SemaphoreType.REGULAR((3,)),
        ],
        compiler_params=pltpu.CompilerParams(
            collective_id=0, has_side_effects=True, vmem_limit_bytes=60 * 1024 * 1024
        ),
        name="swin_block",
    )(x, g1, wqkv, wproj, flat, g2, w1, w2.T)
    return result.transpose(2, 0, 1, 3).reshape(4, 12, 12 * CH)


def solution(mesh):
    in_specs = (P(None, "lat", "lon"), P(), P(), P(), P("lat", None, None, None), P(), P(), P())
    return jax.shard_map(
        shards, mesh=mesh, in_specs=in_specs, out_specs=P(None, "lat", "lon"), check_vma=False
    )
```

```python
import functools

import jax
import jax.numpy as jnp
from jax import lax
from jax.experimental import pallas as pl
from jax.experimental.pallas import tpu as pltpu
from jax.sharding import PartitionSpec as P

MESH = pl.DeviceIdType.MESH
BF16 = jnp.bfloat16
F32 = jnp.float32
CH = 192
HEADS = 6
HD = CH // HEADS
TOK = 144
HALF = TOK // 2
LEVEL = ((1, 2), (3, 0))
NEG = -1000000000.0
LOG2E = 1.4426950408889634


def dot_nt(a, b):
    return lax.dot_general(a, b, (((1,), (1,)), ((), ())), preferred_element_type=F32)


def dot(a, b):
    return jnp.dot(a, b, preferred_element_type=F32)


def row_mean(values):
    mean = dot(values.astype(BF16), jnp.ones((CH, 128), BF16)) * (1.0 / CH)
    return jnp.concatenate([mean, mean[:, : CH - 128]], axis=1)


def layer_norm(values, gain):
    center = values - row_mean(values)
    spread = row_mean(center * center)
    return center * lax.rsqrt(spread + 1e-05) * gain


def block_kernel(
    lons, lats,
    x_hbm, g1_hbm, wqkv_hbm, wproj_hbm, bias_hbm, g2_hbm, w1_hbm, w2t_hbm,
    out,
    xin, raw, lin, blo, bhi, fq, qlo, qhi, stack, qst, frow, xlo, xhi, mixs, rlo, rhi, orow, back,
    g1, g2, wqkv, wproj, w1, w2t,
    load_sem, own_sem, send_sem, recv_sem, ready,
):
    lon = lax.axis_index("lon")
    lat = lax.axis_index("lat")
    east = lax.rem(lon + 1, lons)
    west = lax.rem(lon + lons - 1, lons)
    south = lax.rem(lat + 1, lats)
    north = lax.rem(lat + lats - 1, lats)

    barrier = pltpu.get_barrier_semaphore()
    for a, b in ((west, lat), (lon, north), (west, south), (west, north)):
        pl.semaphore_signal(barrier, inc=1, device_id={"lon": a, "lat": b}, device_id_type=MESH)

    loads = [
        pltpu.make_async_copy(src, dst, load_sem.at[i])
        for i, (src, dst) in enumerate(
            (
                (bias_hbm, raw), (g1_hbm, g1), (wqkv_hbm, wqkv), (wproj_hbm, wproj),
                (g2_hbm, g2), (w1_hbm, w1), (w2t_hbm, w2t),
            )
        )
    ]
    own = [
        pltpu.make_async_copy(x_hbm.at[3:12, 0:9], xin.at[0, 0:9, 9:18], own_sem.at[0]),
        pltpu.make_async_copy(x_hbm.at[3:12, 9:18], xin.at[1, 0:9, 0:9], own_sem.at[1]),
    ]
    for copy in own + loads:
        copy.start()

    def remote(i, src, dst, a, b):
        return pltpu.make_async_remote_copy(
            src_ref=src, dst_ref=dst, send_sem=send_sem.at[i], recv_sem=recv_sem.at[i],
            device_id={"lon": a, "lat": b}, device_id_type=MESH,
        )

    halo = [
        remote(0, x_hbm.at[9:12, 9:18], xin.at[0, 6:9, 0:9], east, lat),
        remote(1, x_hbm.at[0:3, 9:18], xin.at[0, 9:12, 0:9], east, north),
        remote(2, x_hbm.at[3:9, 9:18], xin.at[0, 0:6, 0:9], east, lat),
        remote(3, x_hbm.at[3:9, 0:9], xin.at[1, 0:6, 9:18], west, lat),
        remote(4, x_hbm.at[9:12, 0:9], xin.at[1, 6:9, 9:18], west, lat),
        remote(5, x_hbm.at[0:3, 0:9], xin.at[1, 9:12, 9:18], west, north),
        remote(6, x_hbm.at[0:3, 9:18], xin.at[1, 9:12, 0:9], lon, north),
        remote(7, x_hbm.at[0:3, 0:9], xin.at[0, 9:12, 9:18], lon, north),
    ]
    query_needs = (((), (7,)), ((), (6,)))
    key_needs = (((2,), (0, 1)), ((3,), (4, 5)))

    def give_back(ew):
        columns = pl.ds(9 * ew, 9)
        return remote(8 + ew, back.at[:, columns], out.at[0:3, columns], lon, south)


    pl.semaphore_wait(barrier, 4)
    for i, (a, b) in enumerate(((east, lat), (east, south), (lon, south))):
        pl.semaphore_signal(ready.at[i], inc=1, device_id={"lon": a, "lat": b}, device_id_type=MESH)
    for i in (1, 0, 2):
        halo[i].start()

    def westward():
        pl.semaphore_wait(ready.at[0], 1)
        for i in (4, 3):
            halo[i].start()
        pl.semaphore_wait(ready.at[1], 1)
        halo[5].start()

    loads[0].wait()

    def linear(rh, carry):
        base = pl.multiple_of(rh * 324, 4)
        for t in range(162):
            lin[pl.ds(base + 2 * t, 2), :] = raw[rh, :, 128 * t : 128 * t + 128]
        return carry

    lax.fori_loop(0, 12, linear, 0)

    lanes = lax.broadcasted_iota(jnp.int32, (72, 128), 1)
    place = lax.broadcasted_iota(jnp.int32, (72, 128), 0)
    step = lax.rem(place, 6)
    level_q = step // 3
    last = jnp.where(lat == lats - 1, NEG, 0.0).astype(F32)

    def key_level(key):
        return key // 72

    def key_edge(key):
        return lax.rem(key // 12, 6) // 3

    edge_rows = place >= 36

    def penalty(key, odd, zwin):
        row_q = lax.rem(2 * step + odd, 6) // 3
        pen = jnp.where(jnp.logical_and(edge_rows, row_q != key_edge(key)), last, 0.0)
        if zwin:
            pen = pen + jnp.where(level_q != key_level(key), NEG, 0.0)
        return pen

    for zwin in range(2):
        for odd in range(2):
            pen_lo = penalty(lanes, odd, zwin)
            pen_hi = penalty(lanes + 128, odd, zwin)
            for wc in range(12):
                c = 12 * odd + wc
                start = (9 * (c // 8) + c % 8) * 2 + zwin
                this = lin[pl.ds(start, 72, stride=54), :]
                following = lin[pl.ds(start + 2, 72, stride=54), :]
                turn = 16 * (c % 8)
                if turn:
                    this = pltpu.roll(this, 128 - turn, 1)
                    following = pltpu.roll(following, 128 - turn, 1)
                low = jnp.where(lanes < 128 - turn, this, following)
                dest = (zwin * 2 + wc // 6) * 864 + 6 * odd + wc % 6
                blo[pl.ds(dest, 72, stride=12), :] = low * LOG2E + pen_lo
                bhi[pl.ds(dest, 72, stride=12), :] = jnp.where(lanes < TOK - 128, following * LOG2E + pen_hi, NEG)

    pl.semaphore_wait(ready.at[2], 1)
    for i in (6, 7):
        halo[i].start()
    across = lax.rem(lon, 16) == 0

    for copy in loads[1:]:
        copy.wait()
    for copy in own:
        copy.wait()

    lane36 = lax.broadcasted_iota(jnp.int32, (36, 128), 1)
    lane18 = lax.broadcasted_iota(jnp.int32, (18, 128), 1)

    head_of = lax.broadcasted_iota(jnp.int32, (HALF, CH), 1) // HD

    def queries(rwin, ew):
        own_tiles = pl.ds(9 - 9 * ew, 9)
        tile = xin[ew, 6 * rwin : 6 * rwin + 6, own_tiles].astype(F32)
        fq[rwin * 216 : rwin * 216 + 216, :] = tile.reshape(216, 128)
        for zwin in range(2):
            for lev in range(2):
                base = rwin * 216 + LEVEL[zwin][lev]
                t0 = fq[pl.ds(base, 18, stride=12), :]
                t1 = fq[pl.ds(base + 4, 18, stride=12), :]
                t2 = fq[pl.ds(base + 8, 18, stride=12), :]
                r1 = pltpu.roll(t1, 64, 1)
                r2 = pltpu.roll(t2, 64, 1)
                dest = rwin * TOK + zwin * HALF + 36 * lev
                qlo[pl.ds(dest, 18, stride=2), :] = t0
                qhi[pl.ds(dest, 18, stride=2), :] = t1
                qlo[pl.ds(dest + 1, 18, stride=2), :] = jnp.where(lane18 < 64, r1, r2)
                qhi[pl.ds(dest + 1, 18, stride=2), :] = r2
        normed = layer_norm(tokens(qlo, qhi, rwin * TOK, TOK), g1[...]).astype(BF16)
        query = dot(normed, wqkv[:, :CH]) * (HD ** (-0.5) * LOG2E)
        for zwin in range(2):
            part = query[zwin * HALF : (zwin + 1) * HALF]
            for h in range(HEADS):
                stack[pl.ds(h * HALF, HALF), :] = jnp.where(head_of == h, part, 0.0)
            qst[rwin, zwin] = stack[...].astype(BF16)

    def tokens(low, high, start, size):
        return jnp.concatenate([low[start : start + size, :], high[start : start + size, : CH - 128]], axis=1)

    def attend(rwin, ew):
        tile = xin[ew, 6 * rwin : 6 * rwin + 6].astype(F32)
        frow[rwin * 432 : rwin * 432 + 432, :] = tile.reshape(432, 128)
        for zwin in range(2):
            for lev in range(2):
                base = rwin * 432 + LEVEL[zwin][lev]
                t0 = frow[pl.ds(base, 36, stride=12), :]
                t1 = frow[pl.ds(base + 4, 36, stride=12), :]
                t2 = frow[pl.ds(base + 8, 36, stride=12), :]
                r1 = pltpu.roll(t1, 64, 1)
                r2 = pltpu.roll(t2, 64, 1)
                dest = (rwin * 2 + zwin) * TOK + 72 * lev
                xlo[pl.ds(dest, 36, stride=2), :] = t0
                xhi[pl.ds(dest, 36, stride=2), :] = t1
                xlo[pl.ds(dest + 1, 36, stride=2), :] = jnp.where(lane36 < 64, r1, r2)
                xhi[pl.ds(dest + 1, 36, stride=2), :] = r2
        normed = layer_norm(tokens(xlo, xhi, rwin * 2 * TOK, 2 * TOK), g1[...]).astype(BF16)
        kv = dot(normed, wqkv[:, CH:]).astype(BF16)
        blank = jnp.zeros((256 - TOK, 2 * CH), BF16)
        for zwin in range(2):
            mine = jnp.concatenate([kv[zwin * TOK : (zwin + 1) * TOK], blank], axis=0)
            scores = dot_nt(qst[rwin, zwin], mine[:, :CH])
            brow = pl.ds(pl.multiple_of(((zwin * 2 + 1 - ew) * 2 + rwin) * 432, 8), 432)
            scores = scores + jnp.concatenate([blo[brow, :], bhi[brow, :]], axis=1)
            top = jnp.max(scores, axis=-1, keepdims=True)
            probs = jnp.exp2(scores - top)
            total = jnp.sum(probs, axis=-1, keepdims=True)
            heads = dot(probs.astype(BF16), mine[:, CH:])
            mixed, norm = heads[:HALF], jnp.broadcast_to(total[:HALF], (HALF, CH))
            for h in range(1, HEADS):
                mixed = jnp.where(head_of == h, heads[h * HALF : (h + 1) * HALF], mixed)
                norm = jnp.where(head_of == h, total[h * HALF : (h + 1) * HALF], norm)
            mixs[rwin, zwin * HALF : (zwin + 1) * HALF, :] = mixed / norm

    def finish(rwins, ew):
        first, size = rwins[0] * TOK, len(rwins) * TOK
        mixed = jnp.concatenate([mixs[rwin] for rwin in rwins], axis=0)
        attn = dot(mixed.astype(BF16), wproj[...]).astype(BF16).astype(F32)
        resid = (tokens(qlo, qhi, first, size) + attn).astype(BF16).astype(F32)
        normed = layer_norm(resid, g2[...]).astype(BF16)
        hidden = jax.nn.gelu(dot(normed, w1[...])).astype(BF16)
        result = resid + dot_nt(hidden, w2t[...])
        rlo[first : first + size, :] = result[:, :128]
        rhi[first : first + size, : CH - 128] = result[:, 128:]
        columns = pl.ds(9 * ew, 9)
        for rwin in rwins:
            for zwin in range(2):
                for lev in range(2):
                    base = rwin * TOK + zwin * HALF + 36 * lev
                    even_lo = rlo[pl.ds(base, 18, stride=2), :]
                    even_hi = rhi[pl.ds(base, 18, stride=2), :]
                    odd_lo = pltpu.roll(rlo[pl.ds(base + 1, 18, stride=2), :], 64, 1)
                    odd_hi = pltpu.roll(rhi[pl.ds(base + 1, 18, stride=2), :], 64, 1)
                    dest = rwin * 216 + LEVEL[zwin][lev]
                    orow[pl.ds(dest, 18, stride=12), :] = even_lo
                    orow[pl.ds(dest + 4, 18, stride=12), :] = jnp.where(lane18 < 64, even_hi, odd_lo)
                    orow[pl.ds(dest + 8, 18, stride=12), :] = jnp.where(lane18 < 64, odd_lo, odd_hi)
            tile = orow[rwin * 216 : rwin * 216 + 216, :].reshape(6, 9, 4, 128).astype(BF16)
            if rwin == 0:
                out[3:9, columns] = tile
            else:
                out[9:12, columns] = tile[:3]
                back[:, columns] = tile[3:]
                give_back(ew).start()

    def arrive(which, rwin, ew):
        for side in range(2):

            @pl.when(ew == side)
            def _(side=side):
                for i in which[side][rwin]:
                    halo[i].wait_recv()

    early = jnp.where(across, 1, 0)
    late = 1 - early
    queries(0, early)

    @pl.when(jnp.logical_not(across))
    def _():
        westward()

    for rwin in range(2):
        if rwin:
            arrive(query_needs, rwin, early)
            queries(rwin, early)
        arrive(key_needs, rwin, early)
        attend(rwin, early)
    finish((0, 1), early)
    for rwin in (1, 0):
        arrive(query_needs, rwin, late)
        queries(rwin, late)
    pl.when(across)(westward)
    for rwin in (1, 0):
        arrive(key_needs, rwin, late)
        attend(rwin, late)
        finish((rwin,), late)
    for copy in halo:
        copy.wait_send()
    for ew in range(2):
        give_back(ew).wait()


def shards(field_in, g1, wqkv, wproj, bias, g2, w1, w2):
    lons, lats = lax.axis_size("lon"), lax.axis_size("lat")
    x = field_in.reshape(4, 12, 18, 128).transpose(1, 2, 0, 3)
    flat = bias.transpose(0, 2, 1, 3).reshape(12, 2, 20736)
    hbm = pl.BlockSpec(memory_space=pltpu.MemorySpace.HBM)
    result = pl.pallas_call(
        functools.partial(block_kernel, lons, lats),
        out_shape=pltpu.VMEM((12, 18, 4, 128), BF16),
        in_specs=[hbm] * 8,
        out_specs=pl.BlockSpec(memory_space=pltpu.VMEM),
        scratch_shapes=[
            pltpu.VMEM((2, 12, 18, 4, 128), BF16),
            pltpu.VMEM((12, 2, 20736), F32),
            pltpu.VMEM((3888, 128), F32),
            pltpu.VMEM((3456, 128), F32),
            pltpu.VMEM((3456, 128), F32),
            pltpu.VMEM((432, 128), F32),
            pltpu.VMEM((288, 128), F32),
            pltpu.VMEM((288, 128), F32),
            pltpu.VMEM((432, CH), F32),
            pltpu.VMEM((2, 2, 432, CH), BF16),
            pltpu.VMEM((864, 128), F32),
            pltpu.VMEM((576, 128), F32),
            pltpu.VMEM((576, 128), F32),
            pltpu.VMEM((2, TOK, CH), F32),
            pltpu.VMEM((2 * TOK, 128), F32),
            pltpu.VMEM((2 * TOK, 128), F32),
            pltpu.VMEM((432, 128), F32),
            pltpu.VMEM((3, 18, 4, 128), BF16),
            pltpu.VMEM((CH,), F32),
            pltpu.VMEM((CH,), F32),
            pltpu.VMEM((CH, 3 * CH), BF16),
            pltpu.VMEM((CH, CH), BF16),
            pltpu.VMEM((CH, 768), BF16),
            pltpu.VMEM((CH, 768), BF16),
            pltpu.SemaphoreType.DMA((7,)),
            pltpu.SemaphoreType.DMA((2,)),
            pltpu.SemaphoreType.DMA((10,)),
            pltpu.SemaphoreType.DMA((10,)),
            pltpu.SemaphoreType.REGULAR((3,)),
        ],
        compiler_params=pltpu.CompilerParams(
            collective_id=0, has_side_effects=True, vmem_limit_bytes=60 * 1024 * 1024
        ),
        name="swin_block",
    )(x, g1, wqkv, wproj, flat, g2, w1, w2.T)
    return result.transpose(2, 0, 1, 3).reshape(4, 12, 12 * CH)


def solution(mesh):
    in_specs = (P(None, "lat", "lon"), P(), P(), P(), P("lat", None, None, None), P(), P(), P())
    return jax.shard_map(
        shards, mesh=mesh, in_specs=in_specs, out_specs=P(None, "lat", "lon"), check_vma=False
    )
```

```python
import functools

import jax
import jax.numpy as jnp
from jax import lax
from jax.experimental import pallas as pl
from jax.experimental.pallas import tpu as pltpu
from jax.sharding import PartitionSpec as P

MESH = pl.DeviceIdType.MESH
BF16 = jnp.bfloat16
F32 = jnp.float32
CH = 192
HEADS = 6
HD = CH // HEADS
TOK = 144
HALF = TOK // 2
LEVEL = ((1, 2), (3, 0))
NEG = -1000000000.0
LOG2E = 1.4426950408889634


def dot_nt(a, b):
    return lax.dot_general(a, b, (((1,), (1,)), ((), ())), preferred_element_type=F32)


def dot(a, b):
    return jnp.dot(a, b, preferred_element_type=F32)


def row_mean(values):
    mean = dot(values.astype(BF16), jnp.ones((CH, 128), BF16)) * (1.0 / CH)
    return jnp.concatenate([mean, mean[:, : CH - 128]], axis=1)


def layer_norm(values, gain):
    center = values - row_mean(values)
    spread = row_mean(center * center)
    return center * lax.rsqrt(spread + 1e-05) * gain


def block_kernel(
    lons, lats,
    x_hbm, g1_hbm, wqkv_hbm, wproj_hbm, bias_hbm, g2_hbm, w1_hbm, w2t_hbm,
    out,
    xin, raw, lin, blo, bhi, fq, qlo, qhi, stack, qst, frow, xlo, xhi, mixs, rlo, rhi, orow, back,
    g1, g2, wqkv, wproj, w1, w2t,
    load_sem, own_sem, send_sem, recv_sem, ready,
):
    lon = lax.axis_index("lon")
    lat = lax.axis_index("lat")
    east = lax.rem(lon + 1, lons)
    west = lax.rem(lon + lons - 1, lons)
    south = lax.rem(lat + 1, lats)
    north = lax.rem(lat + lats - 1, lats)

    barrier = pltpu.get_barrier_semaphore()
    for a, b in ((west, lat), (lon, north), (west, south), (west, north)):
        pl.semaphore_signal(barrier, inc=1, device_id={"lon": a, "lat": b}, device_id_type=MESH)

    loads = [
        pltpu.make_async_copy(src, dst, load_sem.at[i])
        for i, (src, dst) in enumerate(
            (
                (bias_hbm, raw), (g1_hbm, g1), (wqkv_hbm, wqkv), (wproj_hbm, wproj),
                (g2_hbm, g2), (w1_hbm, w1), (w2t_hbm, w2t),
            )
        )
    ]
    own = [
        pltpu.make_async_copy(x_hbm.at[3:12, 0:9], xin.at[0, 0:9, 9:18], own_sem.at[0]),
        pltpu.make_async_copy(x_hbm.at[3:12, 9:18], xin.at[1, 0:9, 0:9], own_sem.at[1]),
    ]
    for copy in own + loads:
        copy.start()

    def remote(i, src, dst, a, b):
        return pltpu.make_async_remote_copy(
            src_ref=src, dst_ref=dst, send_sem=send_sem.at[i], recv_sem=recv_sem.at[i],
            device_id={"lon": a, "lat": b}, device_id_type=MESH,
        )

    halo = [
        remote(0, x_hbm.at[9:12, 9:18], xin.at[0, 6:9, 0:9], east, lat),
        remote(1, x_hbm.at[0:3, 9:18], xin.at[0, 9:12, 0:9], east, north),
        remote(2, x_hbm.at[3:9, 9:18], xin.at[0, 0:6, 0:9], east, lat),
        remote(3, x_hbm.at[3:9, 0:9], xin.at[1, 0:6, 9:18], west, lat),
        remote(4, x_hbm.at[9:12, 0:9], xin.at[1, 6:9, 9:18], west, lat),
        remote(5, x_hbm.at[0:3, 0:9], xin.at[1, 9:12, 9:18], west, north),
        remote(6, x_hbm.at[0:3, 9:18], xin.at[1, 9:12, 0:9], lon, north),
        remote(7, x_hbm.at[0:3, 0:9], xin.at[0, 9:12, 9:18], lon, north),
    ]
    query_needs = (((), (7,)), ((), (6,)))
    key_needs = (((2,), (0, 1)), ((3,), (4, 5)))

    def give_back(ew):
        columns = pl.ds(9 * ew, 9)
        return remote(8 + ew, back.at[:, columns], out.at[0:3, columns], lon, south)


    pl.semaphore_wait(barrier, 4)
    for i, (a, b) in enumerate(((east, lat), (east, south), (lon, south))):
        pl.semaphore_signal(ready.at[i], inc=1, device_id={"lon": a, "lat": b}, device_id_type=MESH)
    for i in (1, 0, 2):
        halo[i].start()

    def westward():
        pl.semaphore_wait(ready.at[0], 1)
        for i in (4, 3):
            halo[i].start()
        pl.semaphore_wait(ready.at[1], 1)
        halo[5].start()

    loads[0].wait()

    def linear(rh, carry):
        base = pl.multiple_of(rh * 324, 4)
        for t in range(162):
            lin[pl.ds(base + 2 * t, 2), :] = raw[rh, :, 128 * t : 128 * t + 128]
        return carry

    lax.fori_loop(0, 12, linear, 0)

    lanes = lax.broadcasted_iota(jnp.int32, (72, 128), 1)
    place = lax.broadcasted_iota(jnp.int32, (72, 128), 0)
    step = lax.rem(place, 6)
    level_q = step // 3
    last = jnp.where(lat == lats - 1, NEG, 0.0).astype(F32)

    def key_level(key):
        return key // 72

    def key_edge(key):
        return lax.rem(key // 12, 6) // 3

    edge_rows = place >= 36

    def penalty(key, odd, zwin):
        row_q = lax.rem(2 * step + odd, 6) // 3
        pen = jnp.where(jnp.logical_and(edge_rows, row_q != key_edge(key)), last, 0.0)
        if zwin:
            pen = pen + jnp.where(level_q != key_level(key), NEG, 0.0)
        return pen

    for zwin in range(2):
        for odd in range(2):
            pen_lo = penalty(lanes, odd, zwin)
            pen_hi = penalty(lanes + 128, odd, zwin)
            for wc in range(12):
                c = 12 * odd + wc
                start = (9 * (c // 8) + c % 8) * 2 + zwin
                this = lin[pl.ds(start, 72, stride=54), :]
                following = lin[pl.ds(start + 2, 72, stride=54), :]
                turn = 16 * (c % 8)
                if turn:
                    this = pltpu.roll(this, 128 - turn, 1)
                    following = pltpu.roll(following, 128 - turn, 1)
                low = jnp.where(lanes < 128 - turn, this, following)
                dest = (zwin * 2 + wc // 6) * 864 + 6 * odd + wc % 6
                blo[pl.ds(dest, 72, stride=12), :] = low * LOG2E + pen_lo
                bhi[pl.ds(dest, 72, stride=12), :] = jnp.where(lanes < TOK - 128, following * LOG2E + pen_hi, NEG)

    pl.semaphore_wait(ready.at[2], 1)
    for i in (6, 7):
        halo[i].start()
    across = lax.rem(lon, 16) == 0

    @pl.when(jnp.logical_not(across))
    def _():
        westward()

    for copy in loads[1:]:
        copy.wait()
    for copy in own:
        copy.wait()

    lane36 = lax.broadcasted_iota(jnp.int32, (36, 128), 1)
    lane18 = lax.broadcasted_iota(jnp.int32, (18, 128), 1)

    head_of = lax.broadcasted_iota(jnp.int32, (HALF, CH), 1) // HD

    def queries(rwin, ew):
        own_tiles = pl.ds(9 - 9 * ew, 9)
        tile = xin[ew, 6 * rwin : 6 * rwin + 6, own_tiles].astype(F32)
        fq[rwin * 216 : rwin * 216 + 216, :] = tile.reshape(216, 128)
        for zwin in range(2):
            for lev in range(2):
                base = rwin * 216 + LEVEL[zwin][lev]
                t0 = fq[pl.ds(base, 18, stride=12), :]
                t1 = fq[pl.ds(base + 4, 18, stride=12), :]
                t2 = fq[pl.ds(base + 8, 18, stride=12), :]
                r1 = pltpu.roll(t1, 64, 1)
                r2 = pltpu.roll(t2, 64, 1)
                dest = rwin * TOK + zwin * HALF + 36 * lev
                qlo[pl.ds(dest, 18, stride=2), :] = t0
                qhi[pl.ds(dest, 18, stride=2), :] = t1
                qlo[pl.ds(dest + 1, 18, stride=2), :] = jnp.where(lane18 < 64, r1, r2)
                qhi[pl.ds(dest + 1, 18, stride=2), :] = r2
        normed = layer_norm(tokens(qlo, qhi, rwin * TOK, TOK), g1[...]).astype(BF16)
        query = dot(normed, wqkv[:, :CH]) * (HD ** (-0.5) * LOG2E)
        for zwin in range(2):
            part = query[zwin * HALF : (zwin + 1) * HALF]
            for h in range(HEADS):
                stack[pl.ds(h * HALF, HALF), :] = jnp.where(head_of == h, part, 0.0)
            qst[rwin, zwin] = stack[...].astype(BF16)

    def tokens(low, high, start, size):
        return jnp.concatenate([low[start : start + size, :], high[start : start + size, : CH - 128]], axis=1)

    def attend(rwin, ew):
        tile = xin[ew, 6 * rwin : 6 * rwin + 6].astype(F32)
        frow[rwin * 432 : rwin * 432 + 432, :] = tile.reshape(432, 128)
        for zwin in range(2):
            for lev in range(2):
                base = rwin * 432 + LEVEL[zwin][lev]
                t0 = frow[pl.ds(base, 36, stride=12), :]
                t1 = frow[pl.ds(base + 4, 36, stride=12), :]
                t2 = frow[pl.ds(base + 8, 36, stride=12), :]
                r1 = pltpu.roll(t1, 64, 1)
                r2 = pltpu.roll(t2, 64, 1)
                dest = (rwin * 2 + zwin) * TOK + 72 * lev
                xlo[pl.ds(dest, 36, stride=2), :] = t0
                xhi[pl.ds(dest, 36, stride=2), :] = t1
                xlo[pl.ds(dest + 1, 36, stride=2), :] = jnp.where(lane36 < 64, r1, r2)
                xhi[pl.ds(dest + 1, 36, stride=2), :] = r2
        normed = layer_norm(tokens(xlo, xhi, rwin * 2 * TOK, 2 * TOK), g1[...]).astype(BF16)
        kv = dot(normed, wqkv[:, CH:]).astype(BF16)
        blank = jnp.zeros((256 - TOK, 2 * CH), BF16)
        for zwin in range(2):
            mine = jnp.concatenate([kv[zwin * TOK : (zwin + 1) * TOK], blank], axis=0)
            scores = dot_nt(qst[rwin, zwin], mine[:, :CH])
            brow = pl.ds(pl.multiple_of(((zwin * 2 + 1 - ew) * 2 + rwin) * 432, 8), 432)
            scores = scores + jnp.concatenate([blo[brow, :], bhi[brow, :]], axis=1)
            top = jnp.max(scores, axis=-1, keepdims=True)
            probs = jnp.exp2(scores - top)
            total = jnp.sum(probs, axis=-1, keepdims=True)
            heads = dot(probs.astype(BF16), mine[:, CH:])
            mixed, norm = heads[:HALF], jnp.broadcast_to(total[:HALF], (HALF, CH))
            for h in range(1, HEADS):
                mixed = jnp.where(head_of == h, heads[h * HALF : (h + 1) * HALF], mixed)
                norm = jnp.where(head_of == h, total[h * HALF : (h + 1) * HALF], norm)
            mixs[rwin, zwin * HALF : (zwin + 1) * HALF, :] = mixed / norm

    def finish(rwins, ew):
        first, size = rwins[0] * TOK, len(rwins) * TOK
        mixed = jnp.concatenate([mixs[rwin] for rwin in rwins], axis=0)
        attn = dot(mixed.astype(BF16), wproj[...]).astype(BF16).astype(F32)
        resid = (tokens(qlo, qhi, first, size) + attn).astype(BF16).astype(F32)
        normed = layer_norm(resid, g2[...]).astype(BF16)
        hidden = jax.nn.gelu(dot(normed, w1[...])).astype(BF16)
        result = resid + dot_nt(hidden, w2t[...])
        rlo[first : first + size, :] = result[:, :128]
        rhi[first : first + size, : CH - 128] = result[:, 128:]
        columns = pl.ds(9 * ew, 9)
        for rwin in rwins:
            for zwin in range(2):
                for lev in range(2):
                    base = rwin * TOK + zwin * HALF + 36 * lev
                    even_lo = rlo[pl.ds(base, 18, stride=2), :]
                    even_hi = rhi[pl.ds(base, 18, stride=2), :]
                    odd_lo = pltpu.roll(rlo[pl.ds(base + 1, 18, stride=2), :], 64, 1)
                    odd_hi = pltpu.roll(rhi[pl.ds(base + 1, 18, stride=2), :], 64, 1)
                    dest = rwin * 216 + LEVEL[zwin][lev]
                    orow[pl.ds(dest, 18, stride=12), :] = even_lo
                    orow[pl.ds(dest + 4, 18, stride=12), :] = jnp.where(lane18 < 64, even_hi, odd_lo)
                    orow[pl.ds(dest + 8, 18, stride=12), :] = jnp.where(lane18 < 64, odd_lo, odd_hi)
            tile = orow[rwin * 216 : rwin * 216 + 216, :].reshape(6, 9, 4, 128).astype(BF16)
            if rwin == 0:
                out[3:9, columns] = tile
            else:
                back[:, columns] = tile[3:]
                give_back(ew).start()
                out[9:12, columns] = tile[:3]

    def arrive(which, rwin, ew):
        for side in range(2):

            @pl.when(ew == side)
            def _(side=side):
                for i in which[side][rwin]:
                    halo[i].wait_recv()

    early = jnp.where(across, 1, 0)
    late = 1 - early
    for rwin in range(2):
        arrive(query_needs, rwin, early)
        queries(rwin, early)
        arrive(key_needs, rwin, early)
        attend(rwin, early)
    finish((0, 1), early)
    for rwin in (1, 0):
        arrive(query_needs, rwin, late)
        queries(rwin, late)
    pl.when(across)(westward)
    for rwin in (1, 0):
        arrive(key_needs, rwin, late)
        attend(rwin, late)
        finish((rwin,), late)
    for copy in halo:
        copy.wait_send()
    for ew in range(2):
        give_back(ew).wait()


def shards(field_in, g1, wqkv, wproj, bias, g2, w1, w2):
    lons, lats = lax.axis_size("lon"), lax.axis_size("lat")
    x = field_in.reshape(4, 12, 18, 128).transpose(1, 2, 0, 3)
    flat = bias.transpose(0, 2, 1, 3).reshape(12, 2, 20736)
    hbm = pl.BlockSpec(memory_space=pltpu.MemorySpace.HBM)
    result = pl.pallas_call(
        functools.partial(block_kernel, lons, lats),
        out_shape=pltpu.VMEM((12, 18, 4, 128), BF16),
        in_specs=[hbm] * 8,
        out_specs=pl.BlockSpec(memory_space=pltpu.VMEM),
        scratch_shapes=[
            pltpu.VMEM((2, 12, 18, 4, 128), BF16),
            pltpu.VMEM((12, 2, 20736), F32),
            pltpu.VMEM((3888, 128), F32),
            pltpu.VMEM((3456, 128), F32),
            pltpu.VMEM((3456, 128), F32),
            pltpu.VMEM((432, 128), F32),
            pltpu.VMEM((288, 128), F32),
            pltpu.VMEM((288, 128), F32),
            pltpu.VMEM((432, CH), F32),
            pltpu.VMEM((2, 2, 432, CH), BF16),
            pltpu.VMEM((864, 128), F32),
            pltpu.VMEM((576, 128), F32),
            pltpu.VMEM((576, 128), F32),
            pltpu.VMEM((2, TOK, CH), F32),
            pltpu.VMEM((2 * TOK, 128), F32),
            pltpu.VMEM((2 * TOK, 128), F32),
            pltpu.VMEM((432, 128), F32),
            pltpu.VMEM((3, 18, 4, 128), BF16),
            pltpu.VMEM((CH,), F32),
            pltpu.VMEM((CH,), F32),
            pltpu.VMEM((CH, 3 * CH), BF16),
            pltpu.VMEM((CH, CH), BF16),
            pltpu.VMEM((CH, 768), BF16),
            pltpu.VMEM((CH, 768), BF16),
            pltpu.SemaphoreType.DMA((7,)),
            pltpu.SemaphoreType.DMA((2,)),
            pltpu.SemaphoreType.DMA((10,)),
            pltpu.SemaphoreType.DMA((10,)),
            pltpu.SemaphoreType.REGULAR((3,)),
        ],
        compiler_params=pltpu.CompilerParams(
            collective_id=0, has_side_effects=True, vmem_limit_bytes=60 * 1024 * 1024
        ),
        name="swin_block",
    )(x, g1, wqkv, wproj, flat, g2, w1, w2.T)
    return result.transpose(2, 0, 1, 3).reshape(4, 12, 12 * CH)


def solution(mesh):
    in_specs = (P(None, "lat", "lon"), P(), P(), P(), P("lat", None, None, None), P(), P(), P())
    return jax.shard_map(
        shards, mesh=mesh, in_specs=in_specs, out_specs=P(None, "lat", "lon"), check_vma=False
    )
```
